256 devices in a mesh: slab: 32 (over y, z_lo, core), rows: 8 (over z_hi, x).
Axes of the slice: x: 4, y: 4, z: 8 (z_hi: 2, z_lo: 4; z = z_hi * 4 + z_lo), core: 2. Of those that a mesh axis runs over, the one named last changes fastest.
Arguments:
- volume: bfloat16 [64, 1024, 512], P('rows', 'slab'), may hold values from -6 to 6
- x_frequency: int32 [256, 2, 8], replicated, may hold values from 0 to 4095
- y_frequency: int32 [256, 2, 64], replicated, may hold values from 0 to 4095
- measured: float32 [256, 16, 128], P(('slab', 'rows')), may hold values from -6 to 6
- weights: float32 [256, 16, 64], P(('slab', 'rows')), may hold values from 0.25 to 4
Outputs:
- updated: bfloat16 [64, 1024, 512], P('rows', 'slab')
- residual: float32 [256, 16, 128], P(('slab', 'rows'))
The draws below stay inside these ranges and needn't reach their ends.
Inputs may be any that keep to these rules, and one draw needn't show every extreme that they name: `x_frequency`: indices on a frequency grid of 4096 points. `y_frequency`: indices on a frequency grid of 4096 points.
All inputs are finite; a program needn't handle non-finite values.
Results may differ from the reference program's by a relative error of at most 0.0095.
Values may be sent and summed in bfloat16 or wider, within the bound.
No kernel may reach another device: no remote copies, remote signals or barrier semaphores. Data moves between devices by JAX's collectives and lax.ppermute only.
A program may use at most 64 MiB of HBM per device.

```python
import math
import jax
import jax.numpy as jnp
from jax import lax

Y = 1024
Z = 512
A = 2
KXA = 8
KYA = 64
FINE = 4096
X = 64
KZ = 256
PXA = 16


def place_ends(drawn, rng, low, top_value):
    extent = drawn.shape
    index_at = [jax.random.randint(jax.random.fold_in(rng, axis), (), 0, extent[axis]) for axis in range(len(extent))]
    drawn = drawn.at[tuple(index_at)].set(low)
    longest = extent.index(max(extent))
    index_at[longest] = (index_at[longest] + 1) % extent[longest]
    return drawn.at[tuple(index_at)].set(top_value)


def shard_levels(key, shape, pieces, low, top_value):
    def one(dim, shards_of):
        heights = jax.random.uniform(jax.random.fold_in(jax.random.fold_in(key, 6), dim), (shards_of,), jnp.float32, low / len(pieces), top_value / len(pieces))
        return jnp.repeat(jnp.exp(heights), shape[dim] // shards_of).reshape((-1,) + (1,) * (len(shape) - dim - 1))

    gain = one(*pieces[0])
    for cut in pieces[1:]:
        gain = gain * one(*cut)
    return gain


def scatter_about(rng, shape, width, bound, split=(), kind=jnp.bfloat16):
    level = shard_levels(rng, shape, split, -0.22, 0.18) if split else 1.0
    array = jax.random.normal(rng, shape, jnp.float32) * width * level
    return jnp.minimum(jnp.maximum(array, -bound), bound).astype(kind)


def setup_inputs(seed: int = 0) -> dict:
    streams_of = jax.random.split(jax.random.key(seed), 6)
    return {
        "volume": scatter_about(streams_of[0], (X, Y, Z), 1.0, 6.0, ((0, 8), (1, 32))),
        "x_frequency": place_ends(jax.random.randint(streams_of[1], (KZ, A, KXA), 0, FINE), jax.random.fold_in(streams_of[1], 1), 0, FINE - 1).astype(jnp.int32),
        "y_frequency": place_ends(jax.random.randint(streams_of[2], (KZ, A, KYA), 0, FINE), jax.random.fold_in(streams_of[2], 1), 0, FINE - 1).astype(jnp.int32),
        "measured": scatter_about(streams_of[3], (KZ, PXA, 2 * KYA), 1.0, 6.0, ((0, 256),), jnp.float32),
        "weights": jnp.clip(jnp.exp(math.log(4.0) - 2.7725887 * jax.random.uniform(streams_of[4], (KZ, PXA, KYA), jnp.float32) ** shard_levels(streams_of[4], (KZ, PXA, KYA), ((0, 256),), -0.2, 0.2)), 0.25, 4.0),
    }


HIGHEST = lax.Precision.HIGHEST

def contract(pattern, left, right):
    return jnp.einsum(pattern, left, right, precision=HIGHEST, preferred_element_type=jnp.float32)

def complex_product(pattern, left_real, left_imag, right_real, right_imag):
    out_real = contract(pattern, left_real, right_real) - contract(pattern, left_imag, right_imag)
    out_imag = contract(pattern, left_real, right_imag) + contract(pattern, left_imag, right_real)
    return (out_real, out_imag)

def phase_pair(indices, positions):
    expanded = indices.reshape(indices.shape + (1,) * positions.ndim)
    product = expanded * positions % FINE
    angles = product.astype(jnp.float32) * (2.0 * math.pi / FINE)
    parity = (1 - 2 * (positions % 2)).astype(jnp.float32)
    return (jnp.cos(angles) * parity, -jnp.sin(angles) * parity)

def column_table(length, scale):
    kz_values = jnp.arange(length // 2, dtype=jnp.int32)
    depths = jnp.arange(length, dtype=jnp.int32)
    product = kz_values[:, None] * depths[None, :] % length
    angles = product.astype(jnp.float32) * (2.0 * math.pi / length)
    matrix = jnp.stack([jnp.cos(angles), -jnp.sin(angles)], axis=1) * scale
    return matrix.reshape(length, length).astype(jnp.bfloat16)

def residual_of(points, measured, weights):
    owners = points.shape[0]
    shaped = points.reshape(owners, measured.shape[1], 2, weights.shape[2])
    target = measured.reshape(shaped.shape)
    return (weights[:, :, None, :] * (shaped - target)).reshape(measured.shape)

def reference(volume, x_frequency, y_frequency, measured, weights):
    x_total, y_total, length = volume.shape
    spectral = length // 2
    angle_count = x_frequency.shape[1]
    kx_count = x_frequency.shape[2]
    ky_count = y_frequency.shape[2]
    forward_scale = 1.0 / math.sqrt(x_total * y_total)
    back_scale = 1.0 / math.sqrt(angle_count * kx_count * ky_count)
    columns = volume.reshape(x_total * y_total, length)
    spectrum = jnp.dot(column_table(length, 1.0 / math.sqrt(length)), columns.T, preferred_element_type=jnp.float32).astype(jnp.bfloat16)
    spectrum = spectrum.reshape(spectral, 2, x_total, y_total)
    x_positions = jnp.arange(x_total, dtype=jnp.int32)
    y_positions = jnp.arange(y_total, dtype=jnp.int32)

    def one_plane(inputs):
        plane_block, kx_plane, ky_plane, measured_plane, weight_plane = inputs
        plane_block = plane_block.astype(jnp.float32)
        x_real, x_imag = phase_pair(kx_plane, x_positions)
        y_real, y_imag = phase_pair(ky_plane, y_positions)
        g_real, g_imag = complex_product('ajx,xy->ajy', x_real, x_imag, plane_block[0], plane_block[1])
        f_real, f_imag = complex_product('ajy,aby->ajb', g_real, g_imag, y_real, y_imag)
        points = jnp.stack([f_real, f_imag], axis=2) * forward_scale
        misfit = residual_of(points[None], measured_plane[None], weight_plane[None])[0]
        spread = misfit.reshape(angle_count, kx_count, 2, ky_count)
        h_real, h_imag = complex_product('ajb,aby->ajy', spread[:, :, 0], spread[:, :, 1], y_real, -y_imag)
        p_real, p_imag = complex_product('ajx,ajy->xy', x_real, -x_imag, h_real, h_imag)
        return (misfit, (jnp.stack([p_real, p_imag], axis=0) * back_scale).astype(jnp.bfloat16))
    residual, update = lax.map(one_plane, (spectrum, x_frequency, y_frequency, measured, weights))
    update = update.reshape(length, x_total * y_total)
    correction = jnp.dot(update.T, column_table(length, 1.0 / math.sqrt(spectral)), preferred_element_type=jnp.float32)
    updated = (columns.astype(jnp.float32) - 0.5 * correction).astype(jnp.bfloat16).reshape(volume.shape)
    return (updated, residual)
```

```python
import functools
import math

import jax
import jax.numpy as jnp
import numpy as np
from jax import lax
from jax.experimental import pallas as pl
from jax.experimental.pallas import tpu as pltpu
from jax.sharding import Mesh
from jax.sharding import PartitionSpec as P

FINE = 4096
GRAIN = 32
VMEM_LIMIT = 12 * 2**20
F32 = jnp.float32
BF16 = jnp.bfloat16
PEERS = ("y", "zl", "zh", "x")
SLAB = ("y", "zl", "c")
ROWS = ("zh", "x")


def column_table(length, scale, order):
    depths = np.arange(length, dtype=np.int64)
    angles = (order[:, None] * depths[None, :] % length) * (2.0 * math.pi / length)
    matrix = np.stack([np.cos(angles), -np.sin(angles)], axis=1) * scale
    return matrix.reshape(2 * len(order), length).astype(np.float32).astype(BF16)


def cosine_of_turns(turns):
    part = turns - jnp.floor(turns + 0.5)
    angle = (0.25 - jnp.abs(part)) * (2.0 * math.pi)
    square = angle * angle
    series = -1.0 / 39916800.0
    for term in (362880.0, -5040.0, 120.0, -6.0):
        series = series * square + 1.0 / term
    return angle + angle * square * series


def dot(left, right, left_dim, right_dim):
    dims = (((left_dim,), (right_dim,)), ((), ()))
    return lax.dot_general(left, right, dims, preferred_element_type=F32)


def low_half(shape, axis):
    return lax.broadcasted_iota(jnp.int32, shape, axis) < shape[axis] // 2


def exchange_grains(blocks):
    lane = lax.broadcasted_iota(jnp.int32, blocks[0].shape, blocks[0].ndim - 1)
    axis = blocks[0].ndim - 1
    low = lane < 2 * GRAIN
    even = (lane // GRAIN) % 2 == 0
    first = [None] * 4
    for i in (0, 1):
        a, b = blocks[i], blocks[i + 2]
        first[i] = jnp.where(low, a, pltpu.roll(b, 2 * GRAIN, axis))
        first[i + 2] = jnp.where(low, pltpu.roll(a, 2 * GRAIN, axis), b)
    last = [None] * 4
    for i in (0, 2):
        a, b = first[i], first[i + 1]
        last[i] = jnp.where(even, a, pltpu.roll(b, GRAIN, axis))
        last[i + 1] = jnp.where(even, pltpu.roll(a, 3 * GRAIN, axis), b)
    return last


def transform_kernel(columns_ref, table_ref, out_ref):
    spectrum = dot(table_ref[...], columns_ref[...], 1, 1)
    pairs = spectrum.shape[0] // 8
    near = spectrum[:, :128].reshape(pairs, 8, 128)
    far = spectrum[:, 128:].reshape(pairs, 8, 128)
    low = low_half(near.shape, 1)
    even = jnp.where(low, near, pltpu.roll(far, 4, 1))
    odd = jnp.where(low, pltpu.roll(near, 4, 1), far)
    out_ref[...] = jnp.concatenate([even, odd], axis=1).reshape(out_ref.shape).astype(BF16)


def predict_kernel(scale, planes_ref, y_ref, x_ref, out_ref):
    planes = planes_ref[...].astype(F32).reshape(4, 4, 64, 128)
    blocks = exchange_grains([planes[:, i] for i in range(4)])
    left = jnp.concatenate(
        [jnp.concatenate([b[i] for b in blocks], axis=0) for i in range(4)], axis=1
    ).astype(BF16)
    inner = dot(left, y_ref[...], 1, 0).astype(BF16)
    first = low_half((8, 128), 1)
    for p in range(2):
        parts = jnp.concatenate(
            [inner[:, 256 * p : 256 * p + 128], inner[:, 256 * p + 128 : 256 * p + 256]], axis=0
        )
        points = dot(x_ref[p], parts, 1, 0) * scale
        real, imag = points[:16], points[16:]
        out_ref[p, :8] = jnp.where(first, real[:8], pltpu.roll(imag[:8], 64, 1))
        out_ref[p, 8:] = jnp.where(first, pltpu.roll(real[8:], 64, 1), imag[8:])


def spread_kernel(scale, mine_ref, other_ref, target_ref, y_ref, x_ref, misfit_ref, out_ref):
    first = low_half((8, 128), 1)
    zero = jnp.zeros((8, 128), F32)
    pieces = []
    for p in range(2):
        points = mine_ref[p] + other_ref[p]
        misfit = target_ref[p, 16:] * (points - target_ref[p, :16])
        misfit_ref[p] = misfit
        near, far = misfit[:8], misfit[8:]
        spread = jnp.concatenate(
            [
                jnp.where(first, near, zero),
                jnp.where(first, zero, pltpu.roll(far, 64, 1)),
                jnp.where(first, pltpu.roll(near, 64, 1), zero),
                jnp.where(first, zero, far),
            ],
            axis=0,
        ).astype(BF16)
        inner = dot(x_ref[p], spread, 0, 0)
        pieces += [inner[:256], inner[256:]]
    inner = jnp.concatenate(pieces, axis=1).astype(BF16)
    planes = dot(inner, y_ref[...], 1, 1) * scale
    planes = planes.reshape(4, 64, 512)
    for i in range(4):
        blocks = exchange_grains([planes[q, :, 128 * i : 128 * i + 128] for q in range(4)])
        for g in range(4):
            out_ref[pl.ds((4 * i + g) * 64, 64), :] = blocks[g].astype(BF16)


def update_kernel(planes_ref, columns_ref, table_ref, out_ref):
    planes = planes_ref[...].astype(F32)
    planes = planes.reshape(planes.shape[0] // 16, 16, 128)
    even, odd = planes[:, :8], planes[:, 8:]
    low = low_half(even.shape, 1)
    near = jnp.where(low, even, pltpu.roll(odd, 4, 1)).reshape(-1, 128)
    far = jnp.where(low, pltpu.roll(even, 4, 1), odd).reshape(-1, 128)
    back = jnp.concatenate([near, far], axis=1).astype(BF16)
    correction = dot(back, table_ref[...], 0, 0)
    out_ref[...] = (columns_ref[...].astype(F32) - 0.5 * correction).astype(BF16)


def local_call(kernel, outs, flops, *operands):
    whole = pl.BlockSpec(memory_space=pltpu.VMEM)
    moved = sum(math.prod(a.shape) * a.dtype.itemsize for a in operands)
    return pl.pallas_call(
        kernel,
        out_shape=outs,
        in_specs=[whole] * len(operands),
        out_specs=jax.tree.map(lambda _: whole, outs),
        compiler_params=pltpu.CompilerParams(vmem_limit_bytes=VMEM_LIMIT),
        cost_estimate=pl.CostEstimate(flops=flops, bytes_accessed=moved, transcendentals=0),
    )(*operands)


def shards(volume, x_frequency, y_frequency, measured, weights):
    x_local, y_local, length = volume.shape
    cells = x_local * y_local
    planes = length // 2
    size = {a: lax.axis_size(a) for a in SLAB + ROWS}
    at = {a: lax.axis_index(a) for a in SLAB + ROWS}
    stacks = size["y"] * size["zl"]
    cores = size["c"]
    rows = size["zh"] * size["x"]
    x_total, y_total = x_local * rows, y_local * stacks * cores
    angles, kx_count, ky_count = x_frequency.shape[1], x_frequency.shape[2], y_frequency.shape[2]
    forward_scale = 1.0 / math.sqrt(x_total * y_total)
    back_scale = 1.0 / math.sqrt(angles * kx_count * ky_count)
    columns = volume.reshape(cells, length)
    order = np.arange(planes).reshape(stacks, cores, rows).transpose(0, 2, 1).reshape(-1)
    forward = column_table(length, 1.0 / math.sqrt(length), order)
    inverse = column_table(length, 1.0 / math.sqrt(planes), order)

    def exchange(array):
        peers = stacks * rows
        blocks = array.reshape(peers, array.shape[0] // peers, array.shape[1])
        blocks = lax.all_to_all(blocks, PEERS, split_axis=0, concat_axis=0, tiled=True)
        return blocks.reshape(array.shape)

    swap = [(0, 1), (1, 0)]
    sending = local_call(
        transform_kernel,
        jax.ShapeDtypeStruct((4 * cells, 128), BF16),
        2 * cells * length * length,
        columns,
        forward,
    )

    start = (at["y"] * size["zl"] + at["zl"]) * cores * rows + at["zh"] * size["x"] + at["x"]
    half = FINE // 2

    def of_chip(array):
        taken = lax.dynamic_slice_in_dim(array, start, (cores - 1) * rows + 1, 0)[::rows]
        return (taken + half).astype(F32)

    ky = of_chip(y_frequency).reshape(cores, 1, angles * ky_count)
    ky = jnp.broadcast_to(ky, (cores, 2, angles * ky_count)).reshape(1, -1)
    part = np.tile(np.repeat(np.arange(2), angles * ky_count), cores).reshape(1, -1)
    steps = np.arange(stacks * y_local)
    steps = steps // y_local * (cores * y_local) + steps % y_local
    y_at = jnp.asarray(steps, F32).reshape(-1, 1) + (at["c"] * y_local).astype(F32)
    y_table = cosine_of_turns((ky * y_at + part * (FINE // 4)) * (1.0 / FINE)).astype(BF16)

    kx = of_chip(x_frequency).reshape(cores, 1, angles * kx_count, 1)
    kx = jnp.broadcast_to(kx, (cores, 2, angles * kx_count, 1)).reshape(cores, -1, 1)
    point_part = np.repeat(np.arange(2), angles * kx_count).reshape(1, -1, 1)
    halves = cells // 128
    inside = x_local // halves
    grid = np.indices((2, inside, rows, halves, cores, 2)).reshape(6, 1, 1, -1)
    x_at = grid[2] * x_local + grid[3] * inside + grid[1]
    quarter = 3 * (grid[0] + grid[5]) + point_part
    same = grid[4] == np.arange(cores).reshape(-1, 1, 1)
    x_table = cosine_of_turns((kx * x_at + quarter * (FINE // 4)) * (1.0 / FINE))
    x_table = jnp.where(same, x_table, 0.0).astype(BF16)

    mine = jnp.concatenate([measured[0], jnp.concatenate([weights[0], weights[0]], -1)], 0)
    mine, sending = lax.optimization_barrier((mine, sending))
    other = lax.ppermute(mine, "c", swap)
    received = exchange(sending)
    target = jnp.where(at["c"] == 0, jnp.stack([mine, other]), jnp.stack([other, mine]))

    points = local_call(
        functools.partial(predict_kernel, forward_scale),
        jax.ShapeDtypeStruct((cores,) + measured.shape[1:], F32),
        2 * cells * length * length,
        received,
        y_table,
        x_table,
    )
    others = lax.ppermute(points, "c", swap)
    misfit, sending = local_call(
        functools.partial(spread_kernel, back_scale),
        (jax.ShapeDtypeStruct(points.shape, F32), jax.ShapeDtypeStruct(received.shape, BF16)),
        2 * cells * length * length,
        points,
        others,
        target,
        y_table,
        x_table,
    )
    received = exchange(sending)
    residual = lax.dynamic_slice_in_dim(misfit, at["c"], 1, 0)
    updated = local_call(
        update_kernel,
        jax.ShapeDtypeStruct(columns.shape, BF16),
        2 * cells * length * length,
        received,
        columns,
        inverse,
    )
    return (updated.reshape(volume.shape), residual)


def solution(mesh):
    fine = Mesh(mesh.devices.reshape(4, 4, 2, 2, 4), ("y", "zl", "c", "zh", "x"))
    placed = (
        P(ROWS, SLAB, None),
        P(),
        P(),
        P(SLAB + ROWS, None, None),
        P(SLAB + ROWS, None, None),
    )
    return jax.shard_map(
        shards,
        mesh=fine,
        in_specs=placed,
        out_specs=(P(ROWS, SLAB, None), P(SLAB + ROWS, None, None)),
        check_vma=False,
    )
```

```python
import functools
import math

import jax
import jax.numpy as jnp
import numpy as np
from jax import lax
from jax.experimental import pallas as pl
from jax.experimental.pallas import tpu as pltpu
from jax.sharding import Mesh
from jax.sharding import PartitionSpec as P

FINE = 4096
GRAIN = 32
LANES = 128
CHUNKS = 4
VMEM_LIMIT = 12 * 2**20
VMEM_ALL = 61 * 2**20
F32 = jnp.float32
BF16 = jnp.bfloat16
AXES = {"yh": 2, "yl": 2, "zl": 4, "c": 2, "zh": 2, "xh": 2, "xl": 2}
SLAB = ("yh", "yl", "zl", "c")
ROWS = ("zh", "xh", "xl")
PEERS = ("yl", "zl", "zh", "xl")
TEAM = ("yh", "c", "xh")
PLANES = 8
SWAP = [(0, 1), (1, 0)]


def plane_of(**at):
    number = 0
    for axis in SLAB + ROWS:
        number = number * AXES[axis] + at[axis]
    return number


def column_table(length, scale):
    grid = np.arange(length // 2).reshape([AXES[a] for a in SLAB + ROWS])
    order = grid.transpose([(SLAB + ROWS).index(a) for a in PEERS + TEAM]).reshape(-1)
    depths = np.arange(length, dtype=np.int64)
    angles = (order[:, None] * depths[None, :] % length) * (2.0 * math.pi / length)
    matrix = np.stack([np.cos(angles), -np.sin(angles)], axis=1) * scale
    return matrix.reshape(length, length).astype(np.float32).astype(BF16)


def cosine_of_turns(turns):
    part = turns - jnp.floor(turns + 0.5)
    angle = (0.25 - jnp.abs(part)) * (2.0 * math.pi)
    square = angle * angle
    series = -1.0 / 39916800.0
    for term in (362880.0, -5040.0, 120.0, -6.0):
        series = series * square + 1.0 / term
    return angle + angle * square * series


def dot(left, right, left_dim, right_dim):
    dims = (((left_dim,), (right_dim,)), ((), ()))
    return lax.dot_general(left, right, dims, preferred_element_type=F32)


def iota(shape, axis):
    return lax.broadcasted_iota(jnp.int32, shape, axis)


def exchange_grains(blocks):
    lane = iota(blocks[0].shape, 1)
    low = lane < 2 * GRAIN
    even = (lane & GRAIN) == 0
    first = [None] * 4
    for i in (0, 1):
        a, b = blocks[i], blocks[i + 2]
        first[i] = jnp.where(low, a, pltpu.roll(b, 2 * GRAIN, 1))
        first[i + 2] = jnp.where(low, pltpu.roll(a, 2 * GRAIN, 1), b)
    last = [None] * 4
    for i in (0, 2):
        a, b = first[i], first[i + 1]
        last[i] = jnp.where(even, a, pltpu.roll(b, GRAIN, 1))
        last[i + 1] = jnp.where(even, pltpu.roll(a, 3 * GRAIN, 1), b)
    return last


def transform_kernel(columns_hbm, table_hbm, out_hbm, columns, table, staged, sems, out_sems):
    rows = table.shape[0] // CHUNKS
    first = pltpu.make_async_copy(columns_hbm, columns, sems.at[CHUNKS])
    first.start()
    loads = []
    for i in range(CHUNKS):
        part = pl.ds(i * rows, rows)
        loads.append(pltpu.make_async_copy(table_hbm.at[part], table.at[part], sems.at[i]))
        loads[-1].start()
    first.wait()
    stores = []
    for i in range(CHUNKS):
        loads[i].wait()
        spectrum = dot(table[pl.ds(i * rows, rows), :], columns[...], 1, 1).astype(BF16)
        near = spectrum[:, :LANES].reshape(rows // 16, 16, LANES)
        far = spectrum[:, LANES:].reshape(rows // 16, 16, LANES)
        part = pl.ds(i * 2 * rows, 2 * rows)
        staged[part, :] = jnp.stack([near, far], axis=1).reshape(2 * rows, LANES)
        stores.append(pltpu.make_async_copy(staged.at[part], out_hbm.at[part], out_sems.at[i]))
        stores[-1].start()
    for store in stores:
        store.wait()


def tables_kernel(x_ref, y_ref, x_table_ref, y_table_ref, turned):
    at = {a: lax.axis_index(a) for a in SLAB + ROWS}
    turned[...] = y_ref[...].astype(F32).T
    x_all = x_ref[...].astype(F32)
    lane_plane = iota(x_all.shape, 1)
    lane = iota((32, LANES), 1)
    row = iota((32, LANES), 0)
    x_at = ((lane >> 2) & 1) * 32 + at["xh"] * 16 + ((lane >> 1) & 1) * 8
    x_at = (x_at + (lane & 1) * 4 + ((lane >> 3) & 3)).astype(F32)
    quarter = 3 * ((lane >> 6) + ((lane >> 5) & 1)) + (row >> 4)
    x_shift = (quarter * (FINE // 4)).astype(F32)
    y_in = iota((32, LANES), 0).astype(F32)
    block = iota((8, LANES), 0)
    y_block = at["yh"] * 512 + (block >> 2) * 256 + (block & 3) * 64 + at["c"] * 32
    y_block = y_block.astype(F32)
    for p in range(PLANES):
        plane = plane_of(**{**at, "yh": p >> 2, "c": (p >> 1) & 1, "xh": p & 1})
        kx = jnp.sum(jnp.where(lane_plane == plane, x_all, 0.0), axis=1, keepdims=True)
        kx = jnp.concatenate([kx, kx], axis=0) + FINE / 2.0
        x_table_ref[p] = cosine_of_turns((kx * x_at + x_shift) * (1.0 / FINE)).astype(BF16)
        ky = (turned[pl.ds(plane, 1), :] + FINE / 2.0) * (1.0 / FINE)
        fine = ky * y_in
        fine_real, fine_imag = cosine_of_turns(fine), cosine_of_turns(fine + 0.25)
        coarse = ky * y_block
        coarse_real, coarse_imag = cosine_of_turns(coarse), cosine_of_turns(coarse + 0.25)
        for b in range(8):
            real, imag = coarse_real[b : b + 1], coarse_imag[b : b + 1]
            rows = pl.ds(b * 32, 32)
            y_table_ref[p, rows, :LANES] = (real * fine_real - imag * fine_imag).astype(BF16)
            y_table_ref[p, rows, LANES:] = (real * fine_imag + imag * fine_real).astype(BF16)


def own_plane():
    return (lax.axis_index("yh") * 2 + lax.axis_index("c")) * 2 + lax.axis_index("xh")


def predict_kernel(
    scale, planes_ref, y_ref, x_ref, measured_ref, weights_ref, out_ref, sent_ref, turned
):
    planes = planes_ref[...].astype(F32).reshape(2, 4, LANES, LANES)
    for i in range(2):
        blocks = exchange_grains([planes[i, g] for g in range(4)])
        for q in range(4):
            turned[i, pl.ds(q * LANES, LANES), :] = blocks[q]
    first = iota((8, LANES), 1) < LANES // 2
    for p in range(PLANES):
        left = [
            jnp.concatenate(
                [turned[i, pl.ds(2 * p + part, 32, stride=16), :] for i in range(2)], axis=1
            )
            for part in range(2)
        ]
        left = jnp.concatenate(left, axis=0).astype(BF16)
        inner = dot(left, y_ref[p], 1, 0).astype(BF16)
        inner = jnp.concatenate([inner[:, :LANES], inner[:, LANES:]], axis=0)
        points = dot(x_ref[p], inner, 1, 0) * scale
        real, imag = points[:16], points[16:]
        out_ref[p, :8] = jnp.where(first, real[:8], pltpu.roll(imag[:8], 64, 1))
        out_ref[p, 8:16] = jnp.where(first, pltpu.roll(real[8:], 64, 1), imag[8:])
        out_ref[p, 16:] = jnp.zeros((8, LANES), F32)
    own = own_plane()
    out_ref[own, :16] = out_ref[own, :16] - measured_ref[...]
    out_ref[own, 16:] = weights_ref[...]
    sent_ref[...] = out_ref[...].astype(BF16)


def spread_kernel(
    scale, sum_ref, other_ref, y_ref, x_ref, misfit_ref, out_hbm, turned, staged, sems
):
    first = iota((8, LANES), 1) < LANES // 2

    def misfit_of(total):
        near, far, weight = total[:8], total[8:16], total[16:]
        crossed = pltpu.roll(weight, 64, 1)
        return (
            near * jnp.where(first, weight, crossed),
            far * jnp.where(first, crossed, weight),
        )

    zero = jnp.zeros((8, LANES), F32)
    for p in range(PLANES):
        near, far = misfit_of(sum_ref[p] + other_ref[p].astype(F32))
        spread = jnp.concatenate(
            [
                jnp.where(first, near, zero),
                jnp.where(first, zero, pltpu.roll(far, 64, 1)),
                jnp.where(first, pltpu.roll(near, 64, 1), zero),
                jnp.where(first, zero, far),
            ],
            axis=0,
        ).astype(BF16)
        inner = dot(x_ref[p], spread, 0, 0).astype(BF16)
        inner = jnp.concatenate([inner[:64], inner[64:]], axis=1)
        planes = dot(inner, y_ref[p], 1, 1) * scale
        for part in range(2):
            for i in range(2):
                turned[i, pl.ds(2 * p + part, 32, stride=16), :] = planes[
                    part * 32 : part * 32 + 32, i * LANES : i * LANES + LANES
                ]
    stores = []
    for i in range(2):
        blocks = exchange_grains([turned[i, pl.ds(q * LANES, LANES), :] for q in range(4)])
        for g in range(4):
            staged[pl.ds((4 * i + g) * LANES, LANES), :] = blocks[g].astype(BF16)
        part = pl.ds(i * 4 * LANES, 4 * LANES)
        stores.append(pltpu.make_async_copy(staged.at[part], out_hbm.at[part], sems.at[i]))
        stores[-1].start()
    own = own_plane()
    near, far = misfit_of(sum_ref[own] + other_ref[own].astype(F32))
    misfit_ref[:8], misfit_ref[8:] = near, far
    for store in stores:
        store.wait()


def update_kernel(planes_ref, columns_ref, table_ref, out_hbm, staged, sems):
    planes = planes_ref[...].reshape(planes_ref.shape[0] // 32, 2, 16, LANES)
    table = table_ref[...]
    stores = []
    for i in range(2):
        part = pl.ds(i * LANES, LANES)
        correction = dot(planes[:, i].reshape(-1, LANES), table, 0, 0)
        staged[part, :] = (columns_ref[part, :].astype(F32) - 0.5 * correction).astype(BF16)
        stores.append(pltpu.make_async_copy(staged.at[part], out_hbm.at[part], sems.at[i]))
        stores[-1].start()
    for store in stores:
        store.wait()


VMEM = pl.BlockSpec(memory_space=pltpu.VMEM)
HBM = pl.BlockSpec(memory_space=pltpu.HBM)


def local_call(kernel, outs, scratch, operands, specs=None, out_specs=None, limit=VMEM_LIMIT):
    moved = sum(math.prod(a.shape) * a.dtype.itemsize for a in operands)
    return pl.pallas_call(
        kernel,
        out_shape=outs,
        in_specs=specs or [VMEM] * len(operands),
        out_specs=jax.tree.map(lambda _: VMEM, outs) if out_specs is None else out_specs,
        scratch_shapes=scratch,
        compiler_params=pltpu.CompilerParams(vmem_limit_bytes=limit),
        cost_estimate=pl.CostEstimate(flops=2**27, bytes_accessed=moved, transcendentals=0),
    )(*operands)


def shape_of(*shape, dtype=BF16):
    return jax.ShapeDtypeStruct(shape, dtype)


def exchange(array):
    peers = math.prod(AXES[a] for a in PEERS)
    blocks = array.reshape(peers, array.shape[0] // peers, array.shape[1])
    blocks = lax.all_to_all(blocks, PEERS, split_axis=0, concat_axis=0, tiled=True)
    return blocks.reshape(array.shape)


def shards(volume, x_frequency, y_frequency, measured, weights):
    x_local, y_local, length = volume.shape
    cells = x_local * y_local
    rows = cells * length // LANES
    planes, angles, kx_count = x_frequency.shape
    ky_count = y_frequency.shape[2]
    cells_total = cells * math.prod(AXES.values())
    forward_scale = 1.0 / math.sqrt(cells_total)
    back_scale = 1.0 / math.sqrt(angles * kx_count * ky_count)
    columns = volume.reshape(cells, length)
    forward = column_table(length, 1.0 / math.sqrt(length))
    inverse = column_table(length, 1.0 / math.sqrt(planes))

    sending = local_call(
        transform_kernel,
        shape_of(rows, LANES),
        [
            pltpu.VMEM((cells, length), BF16),
            pltpu.VMEM((length, length), BF16),
            pltpu.VMEM((rows, LANES), BF16),
            pltpu.SemaphoreType.DMA((CHUNKS + 1,)),
            pltpu.SemaphoreType.DMA((CHUNKS,)),
        ],
        (columns, forward),
        [HBM, HBM],
        HBM,
        VMEM_ALL,
    )
    received = exchange(sending)

    x_table, y_table = local_call(
        tables_kernel,
        (shape_of(PLANES, 32, LANES), shape_of(PLANES, 256, 256)),
        [pltpu.VMEM((planes, LANES), F32)],
        (
            x_frequency.transpose(1, 2, 0).reshape(angles * kx_count, planes),
            y_frequency.transpose(1, 2, 0).reshape(angles * ky_count, planes),
        ),
    )
    packed = jnp.concatenate([weights[0, :kx_count], weights[0, kx_count:]], axis=-1)
    packed, sending = lax.optimization_barrier((packed, sending))

    work = shape_of(PLANES, 24, LANES, dtype=F32)
    turned = pltpu.VMEM((2, 4 * LANES, LANES), F32)
    total, sent = local_call(
        functools.partial(predict_kernel, forward_scale),
        (work, shape_of(PLANES, 24, LANES)),
        [turned],
        (received, y_table, x_table, measured[0], packed),
    )
    total = total + lax.ppermute(sent, "c", SWAP).astype(F32)
    total = total + lax.ppermute(total.astype(BF16), "xh", SWAP).astype(F32)
    other = lax.ppermute(total.astype(BF16), "yh", SWAP)
    misfit, sending = local_call(
        functools.partial(spread_kernel, back_scale),
        (shape_of(angles * kx_count, LANES, dtype=F32), shape_of(rows, LANES)),
        [turned, pltpu.VMEM((rows, LANES), BF16), pltpu.SemaphoreType.DMA((2,))],
        (total, other, y_table, x_table),
        None,
        (VMEM, HBM),
    )
    received = exchange(sending)
    updated = local_call(
        update_kernel,
        shape_of(cells, length),
        [pltpu.VMEM((cells, length), BF16), pltpu.SemaphoreType.DMA((2,))],
        (received, columns, inverse),
        None,
        HBM,
    )
    return (updated.reshape(volume.shape), misfit.reshape(measured.shape))


def solution(mesh):
    fine = Mesh(mesh.devices.reshape(tuple(AXES.values())), tuple(AXES))
    placed = (
        P(ROWS, SLAB, None),
        P(),
        P(),
        P(SLAB + ROWS, None, None),
        P(SLAB + ROWS, None, None),
    )
    return jax.shard_map(
        shards,
        mesh=fine,
        in_specs=placed,
        out_specs=(P(ROWS, SLAB, None), P(SLAB + ROWS, None, None)),
        check_vma=False,
    )
```

```python
import functools
import math

import jax
import jax.numpy as jnp
import numpy as np
from jax import lax
from jax.experimental import pallas as pl
from jax.experimental.pallas import tpu as pltpu
from jax.sharding import Mesh
from jax.sharding import PartitionSpec as P

FINE = 4096
GRAIN = 32
LANES = 128
VMEM_LIMIT = 12 * 2**20
F32 = jnp.float32
BF16 = jnp.bfloat16
AXES = {"y": 4, "zl": 4, "c": 2, "zh": 2, "x": 4}
SLAB = ("y", "zl", "c")
ROWS = ("zh", "x")
PEERS = ("zl", "y", "x", "zh")
TEAM = ("c",)
PLANES = 2
SWAP = [(0, 1), (1, 0)]


def plane_of(**at):
    number = 0
    for axis in SLAB + ROWS:
        number = number * AXES[axis] + at[axis]
    return number


def column_table(length, scale):
    grid = np.arange(length // 2).reshape([AXES[a] for a in SLAB + ROWS])
    order = grid.transpose([(SLAB + ROWS).index(a) for a in PEERS + TEAM]).reshape(-1)
    depths = np.arange(length, dtype=np.int64)
    angles = (order[:, None] * depths[None, :] % length) * (2.0 * math.pi / length)
    matrix = np.stack([np.cos(angles), -np.sin(angles)], axis=1) * scale
    return matrix.reshape(length, length).astype(np.float32).astype(BF16)


def cosine_of_turns(turns):
    part = turns - jnp.floor(turns + 0.5)
    angle = (0.25 - jnp.abs(part)) * (2.0 * math.pi)
    square = angle * angle
    series = -1.0 / 39916800.0
    for term in (362880.0, -5040.0, 120.0, -6.0):
        series = series * square + 1.0 / term
    return angle + angle * square * series


def dot(left, right, left_dim, right_dim):
    dims = (((left_dim,), (right_dim,)), ((), ()))
    return lax.dot_general(left, right, dims, preferred_element_type=F32)


def iota(shape, axis):
    return lax.broadcasted_iota(jnp.int32, shape, axis)


def exchange_grains(blocks):
    lane = iota(blocks[0].shape, 1)
    low = lane < 2 * GRAIN
    even = (lane & GRAIN) == 0
    first = [None] * 4
    for i in (0, 1):
        a, b = blocks[i], blocks[i + 2]
        first[i] = jnp.where(low, a, pltpu.roll(b, 2 * GRAIN, 1))
        first[i + 2] = jnp.where(low, pltpu.roll(a, 2 * GRAIN, 1), b)
    last = [None] * 4
    for i in (0, 2):
        a, b = first[i], first[i + 1]
        last[i] = jnp.where(even, a, pltpu.roll(b, GRAIN, 1))
        last[i + 1] = jnp.where(even, pltpu.roll(a, 3 * GRAIN, 1), b)
    return last


def forward_kernel(scale, out_ref):
    length = out_ref.shape[1]
    low = (32, length)
    row, depth = iota(low, 0), iota(low, 1)
    plane = ((row >> 1) & 1) * 8 + ((row >> 2) & 1) * 4 + (row >> 3)
    low_real = (plane * depth).astype(F32) * (1.0 / length) + (row & 1).astype(F32) * 0.25
    low_real, low_imag = cosine_of_turns(low_real), cosine_of_turns(low_real + 0.25)
    row, depth = iota((16, length), 0), iota((16, length), 1)
    plane = ((row & 3) * 4 + (row >> 2)) * 16
    high = (plane * depth).astype(F32) * (1.0 / length)
    high_real, high_imag = cosine_of_turns(high) * scale, cosine_of_turns(high + 0.25) * scale
    for b in range(16):
        real, imag = high_real[b : b + 1], high_imag[b : b + 1]
        out_ref[pl.ds(b * 32, 32), :] = (real * low_real - imag * low_imag).astype(BF16)


def tables_kernel(x_ref, y_ref, after_ref, x_table_ref, y_table_ref, turned):
    at = {a: lax.axis_index(a) for a in SLAB + ROWS}
    turned[...] = y_ref[...].astype(F32).T
    x_all = x_ref[...].astype(F32)
    lane_plane = iota(x_all.shape, 1)
    shape = (32, 4 * LANES)
    lane = iota(shape, 1)
    x_at = ((lane >> 3) & 1) * 32 + ((lane >> 4) & 3) * 8 + ((lane >> 2) & 1) * 4
    x_at = (x_at + ((lane >> 6) & 3)).astype(F32)
    quarter = 3 * ((lane >> 8) + (lane & 1)) + (iota(shape, 0) >> 4)
    x_shift = (quarter * (FINE // 4)).astype(F32)
    team = (lane >> 1) & 1
    y_in = iota((32, LANES), 0).astype(F32)
    y_block = (iota((16, LANES), 0) * 64 + at["c"] * 32).astype(F32)
    for p in range(PLANES):
        plane = plane_of(**{**at, "c": p})
        kx = jnp.sum(jnp.where(lane_plane == plane, x_all, 0.0), axis=1, keepdims=True)
        kx = jnp.concatenate([kx, kx], axis=0) + FINE / 2.0
        phase = cosine_of_turns((kx * x_at + x_shift) * (1.0 / FINE))
        x_table_ref[p] = jnp.where(team == p, phase, 0.0).astype(BF16)
        ky = (turned[pl.ds(plane, 1), :] + FINE / 2.0) * (1.0 / FINE)
        fine = ky * y_in
        fine_real, fine_imag = cosine_of_turns(fine), cosine_of_turns(fine + 0.25)
        coarse = ky * y_block
        coarse_real, coarse_imag = cosine_of_turns(coarse), cosine_of_turns(coarse + 0.25)
        for b in range(16):
            real, imag = coarse_real[b : b + 1], coarse_imag[b : b + 1]
            rows = pl.ds(b * 32, 32)
            near, far = pl.ds(2 * p * LANES, LANES), pl.ds((2 * p + 1) * LANES, LANES)
            y_table_ref[rows, near] = (real * fine_real - imag * fine_imag).astype(BF16)
            y_table_ref[rows, far] = (real * fine_imag + imag * fine_real).astype(BF16)


def transform_kernel(columns_ref, table_ref, out_ref):
    spectrum = dot(table_ref[...], columns_ref[...], 1, 1)
    pairs = spectrum.shape[0] // 8
    near = spectrum[:, :LANES].reshape(pairs, 8, LANES)
    far = spectrum[:, LANES:].reshape(pairs, 8, LANES)
    low = iota(near.shape, 1) < 4
    even = jnp.where(low, near, pltpu.roll(far, 4, 1))
    odd = jnp.where(low, pltpu.roll(near, 4, 1), far)
    out_ref[...] = jnp.concatenate([even, odd], axis=1).reshape(out_ref.shape).astype(BF16)


def predict_kernel(scale, planes_ref, y_ref, x_ref, measured_ref, weights_ref, out_ref):
    quarter = planes_ref.shape[0] // 4
    blocks = [planes_ref[pl.ds(g * quarter, quarter), :].astype(F32) for g in range(4)]
    blocks = exchange_grains(blocks)
    rows = quarter // 4
    left = jnp.concatenate(
        [
            jnp.concatenate([b[i * rows : i * rows + rows] for b in blocks], axis=0)
            for i in range(4)
        ],
        axis=1,
    ).astype(BF16)
    inner = dot(left, y_ref[...], 1, 0).astype(BF16)
    first = iota((8, LANES), 1) < LANES // 2
    for p in range(PLANES):
        near = inner[:, 2 * p * LANES : (2 * p + 1) * LANES]
        far = inner[:, (2 * p + 1) * LANES : (2 * p + 2) * LANES]
        points = dot(x_ref[p], jnp.concatenate([near, far], axis=0), 1, 0) * scale
        real, imag = points[:16], points[16:]
        out_ref[p, :8] = jnp.where(first, real[:8], pltpu.roll(imag[:8], 64, 1))
        out_ref[p, 8:16] = jnp.where(first, pltpu.roll(real[8:], 64, 1), imag[8:])
        out_ref[p, 16:] = jnp.zeros((16, LANES), F32)
    own = lax.axis_index("c")
    out_ref[own, :16] = out_ref[own, :16] - measured_ref[...]
    out_ref[own, 16:, : LANES // 2] = weights_ref[...]


def spread_kernel(scale, mine_ref, other_ref, y_ref, x_ref, misfit_ref, out_ref):
    first = iota((8, LANES), 1) < LANES // 2
    zero = jnp.zeros((8, LANES), F32)

    def both(weight):
        return jnp.where(first, weight, pltpu.roll(weight, 64, 1))

    def misfit_of(total):
        return total[:8] * both(total[16:24]), total[8:16] * both(total[24:])

    pieces = []
    for p in range(PLANES):
        near, far = misfit_of(mine_ref[p] + other_ref[p])
        spread = jnp.concatenate(
            [
                jnp.where(first, near, zero),
                jnp.where(first, zero, pltpu.roll(far, 64, 1)),
                jnp.where(first, pltpu.roll(near, 64, 1), zero),
                jnp.where(first, zero, far),
            ],
            axis=0,
        ).astype(BF16)
        inner = dot(x_ref[p], spread, 0, 0).astype(BF16)
        half = inner.shape[0] // 2
        pieces += [inner[:half], inner[half:]]
    planes = dot(jnp.concatenate(pieces, axis=1), y_ref[...], 1, 1) * scale
    rows = planes.shape[0] // 4
    for i in range(4):
        lanes = slice(i * LANES, i * LANES + LANES)
        blocks = [planes[q * rows : q * rows + rows, lanes] for q in range(4)]
        blocks = exchange_grains(blocks)
        for g in range(4):
            out_ref[pl.ds((4 * g + i) * rows, rows), :] = blocks[g].astype(BF16)
    own = lax.axis_index("c")
    near, far = misfit_of(mine_ref[own] + other_ref[own])
    misfit_ref[:8], misfit_ref[8:] = near, far


def update_kernel(planes_ref, columns_ref, table_ref, out_hbm, staged, sems):
    planes = planes_ref[...].astype(F32)
    planes = planes.reshape(planes.shape[0] // 16, 16, LANES)
    even, odd = planes[:, :8], planes[:, 8:]
    low = iota(even.shape, 1) < 4
    near = jnp.where(low, even, pltpu.roll(odd, 4, 1)).reshape(-1, LANES).astype(BF16)
    far = jnp.where(low, pltpu.roll(even, 4, 1), odd).reshape(-1, LANES).astype(BF16)
    table = table_ref[...]
    stores = []
    for i, back in enumerate((near, far)):
        part = pl.ds(i * LANES, LANES)
        correction = dot(back, table, 0, 0)
        staged[part, :] = (columns_ref[part, :].astype(F32) - 0.5 * correction).astype(BF16)
        stores.append(pltpu.make_async_copy(staged.at[part], out_hbm.at[part], sems.at[i]))
        stores[-1].start()
    for store in stores:
        store.wait()


VMEM = pl.BlockSpec(memory_space=pltpu.VMEM)
ANY = pl.BlockSpec(memory_space=pl.ANY)


def local_call(kernel, outs, operands, scratch=(), specs=None, out_specs=None, flops=2**27):
    return pl.pallas_call(
        kernel,
        out_shape=outs,
        in_specs=specs or [VMEM] * len(operands),
        out_specs=jax.tree.map(lambda _: VMEM, outs) if out_specs is None else out_specs,
        scratch_shapes=scratch,
        compiler_params=pltpu.CompilerParams(vmem_limit_bytes=VMEM_LIMIT),
        cost_estimate=pl.CostEstimate(flops=flops, bytes_accessed=flops // 128, transcendentals=0),
    )(*operands)


def shape_of(*shape, dtype=BF16):
    return jax.ShapeDtypeStruct(shape, dtype)


def exchange(array):
    peers = math.prod(AXES[a] for a in PEERS)
    blocks = array.reshape(peers, array.shape[0] // peers, array.shape[1])
    blocks = lax.all_to_all(blocks, PEERS, split_axis=0, concat_axis=0, tiled=True)
    return blocks.reshape(array.shape)


def shards(volume, x_frequency, y_frequency, measured, weights):
    x_local, y_local, length = volume.shape
    cells = x_local * y_local
    rows = cells * length // LANES
    planes, angles, kx_count = x_frequency.shape
    ky_count = y_frequency.shape[2]
    forward_scale = 1.0 / math.sqrt(cells * math.prod(AXES.values()))
    back_scale = 1.0 / math.sqrt(angles * kx_count * ky_count)
    columns = volume.reshape(cells, length)
    forward = local_call(
        functools.partial(forward_kernel, 1.0 / math.sqrt(length)),
        shape_of(length, length),
        (),
        flops=2**10,
    )
    inverse = column_table(length, 1.0 / math.sqrt(planes))

    sending = local_call(
        transform_kernel,
        shape_of(rows, LANES),
        (columns, forward),
    )
    x_table, y_table = local_call(
        tables_kernel,
        (shape_of(PLANES, 32, 4 * LANES), shape_of(4 * LANES, 4 * LANES)),
        (
            x_frequency.transpose(1, 2, 0).reshape(angles * kx_count, planes),
            y_frequency.transpose(1, 2, 0).reshape(angles * ky_count, planes),
            sending,
        ),
        [pltpu.VMEM((planes, LANES), F32)],
        [VMEM, VMEM, ANY],
        flops=2**10,
    )
    x_table, y_table, sending = lax.optimization_barrier((x_table, y_table, sending))
    received = exchange(sending)
    points = local_call(
        functools.partial(predict_kernel, forward_scale),
        shape_of(PLANES, 32, LANES, dtype=F32),
        (received, y_table, x_table, measured[0], weights[0]),
    )
    others = lax.ppermute(points, "c", SWAP)
    misfit, sending = local_call(
        functools.partial(spread_kernel, back_scale),
        (shape_of(angles * kx_count, LANES, dtype=F32), shape_of(rows, LANES)),
        (points, others, y_table, x_table),
    )
    received = exchange(sending)
    updated = local_call(
        update_kernel,
        shape_of(cells, length),
        (received, columns, inverse),
        [pltpu.VMEM((cells, length), BF16), pltpu.SemaphoreType.DMA((2,))],
        out_specs=ANY,
    )
    return (updated.reshape(volume.shape), misfit.reshape(measured.shape))


def solution(mesh):
    fine = Mesh(mesh.devices.reshape(tuple(AXES.values())), tuple(AXES))
    placed = (
        P(ROWS, SLAB, None),
        P(),
        P(),
        P(SLAB + ROWS, None, None),
        P(SLAB + ROWS, None, None),
    )
    return jax.shard_map(
        shards,
        mesh=fine,
        in_specs=placed,
        out_specs=(P(ROWS, SLAB, None), P(SLAB + ROWS, None, None)),
        check_vma=False,
    )
```

```python
import functools
import math

import jax
import jax.numpy as jnp
import numpy as np
from jax import lax
from jax.experimental import pallas as pl
from jax.experimental.pallas import tpu as pltpu
from jax.sharding import Mesh
from jax.sharding import PartitionSpec as P

FINE = 4096
GRAIN = 32
LANES = 128
VMEM_LIMIT = 12 * 2**20
START_LIMIT = 12 * 2**20
F32 = jnp.float32
BF16 = jnp.bfloat16
AXES = {"y": 4, "zl": 4, "c": 2, "zh": 2, "x": 4}
SLAB = ("y", "zl", "c")
ROWS = ("zh", "x")
OUT = ("zl", "y", "x", "zh")
BACK = ("zl", "y", "x", "zh")
TEAM = ("c",)
PLANES = 2
SWAP = [(0, 1), (1, 0)]


def bits_of(axes):
    return [
        (a, 1 << b) for a in axes for b in reversed(range(AXES[a].bit_length() - 1))
    ]


PLANE_STEP = {"y": 64, "zl": 16, "c": 8, "zh": 4, "x": 1}
X_STEP = {"zh": 32, "x": 8}
CROSS = tuple(a for a in OUT if a in X_STEP)


def weighted(index, steps):
    total = 0
    for place, step in enumerate(reversed(steps)):
        if step:
            total = total + ((index >> place) & 1) * step
    return total


def runs(peers, **fixed):
    found = []
    for at in np.ndindex(*[AXES[a] for a in CROSS]):
        at = {**fixed, **dict(zip(CROSS, at))}
        peer = 0
        for axis in peers:
            peer = peer * AXES[axis] + at[axis]
        if found and sum(found[-1]) == peer:
            found[-1] = (found[-1][0], found[-1][1] + 1)
        else:
            found.append((int(peer), 1))
    return found


def plane_of(**at):
    number = 0
    for axis in SLAB + ROWS:
        number = number * AXES[axis] + at[axis]
    return number


def column_table(length, scale, peers):
    grid = np.arange(length // 2).reshape([AXES[a] for a in SLAB + ROWS])
    order = grid.transpose([(SLAB + ROWS).index(a) for a in peers + TEAM]).reshape(-1)
    depths = np.arange(length, dtype=np.int64)
    angles = (order[:, None] * depths[None, :] % length) * (2.0 * math.pi / length)
    matrix = np.stack([np.cos(angles), -np.sin(angles)], axis=1) * scale
    return matrix.reshape(length, length).astype(np.float32).astype(BF16)


def cosine_of_turns(turns):
    part = turns - jnp.floor(turns + 0.5)
    angle = (0.25 - jnp.abs(part)) * (2.0 * math.pi)
    square = angle * angle
    series = -1.0 / 39916800.0
    for term in (362880.0, -5040.0, 120.0, -6.0):
        series = series * square + 1.0 / term
    return angle + angle * square * series


def dot(left, right, left_dim, right_dim):
    dims = (((left_dim,), (right_dim,)), ((), ()))
    return lax.dot_general(left, right, dims, preferred_element_type=F32)


def iota(shape, axis):
    return lax.broadcasted_iota(jnp.int32, shape, axis)


def exchange_grains(blocks):
    lane = iota(blocks[0].shape, 1)
    low = lane < 2 * GRAIN
    even = (lane & GRAIN) == 0
    first = [None] * 4
    for i in (0, 1):
        a, b = blocks[i], blocks[i + 2]
        first[i] = jnp.where(low, a, pltpu.roll(b, 2 * GRAIN, 1))
        first[i + 2] = jnp.where(low, pltpu.roll(a, 2 * GRAIN, 1), b)
    last = [None] * 4
    for i in (0, 2):
        a, b = first[i], first[i + 1]
        last[i] = jnp.where(even, a, pltpu.roll(b, GRAIN, 1))
        last[i + 1] = jnp.where(even, pltpu.roll(a, 3 * GRAIN, 1), b)
    return last


def start_kernel(
    x_hbm,
    y_hbm,
    columns_hbm,
    forward_hbm,
    measured_hbm,
    weights_hbm,
    out_ref,
    own_ref,
    x_table_ref,
    y_table_ref,
    x_own,
    y_all,
    columns,
    forward,
    measured,
    weights,
    turned,
    sems,
):
    pairs = (
        (x_hbm, x_own),
        (y_hbm, y_all),
        (columns_hbm, columns),
        (forward_hbm, forward),
        (measured_hbm, measured),
        (weights_hbm, weights),
    )
    loads = [pltpu.make_async_copy(a, b, sems.at[i]) for i, (a, b) in enumerate(pairs)]
    for load in loads:
        load.start()
    at = {a: lax.axis_index(a) for a in SLAB + ROWS}
    for load in loads[:2]:
        load.wait()
    turned[...] = y_all[...].astype(F32).T
    x_all = x_own[...].astype(F32)
    lane_plane = iota(x_all.shape, 1)
    shape = (32, 4 * LANES)
    lane = iota(shape, 1)
    steps = [X_STEP[a] * value for a, value in bits_of(CROSS)]
    x_at = weighted(lane, [0, 2, 1] + steps + [4, 0, 0]).astype(F32)
    quarter = 3 * ((lane >> 8) + (lane & 1)) + (iota(shape, 0) >> 4)
    x_shift = (quarter * (FINE // 4)).astype(F32)
    team = (lane >> 1) & 1
    y_in = iota((32, LANES), 0).astype(F32)
    y_block = (iota((16, LANES), 0) * 64 + at["c"] * 32).astype(F32)
    for p in range(PLANES):
        plane = plane_of(**{**at, "c": p})
        kx = jnp.sum(jnp.where(lane_plane == plane, x_all, 0.0), axis=1, keepdims=True)
        kx = jnp.concatenate([kx, kx], axis=0) + FINE / 2.0
        phase = cosine_of_turns((kx * x_at + x_shift) * (1.0 / FINE))
        x_table_ref[p] = jnp.where(team == p, phase, 0.0).astype(BF16)
        ky = (turned[pl.ds(plane, 1), :] + FINE / 2.0) * (1.0 / FINE)
        fine = ky * y_in
        fine_real, fine_imag = cosine_of_turns(fine), cosine_of_turns(fine + 0.25)
        coarse = ky * y_block
        coarse_real, coarse_imag = cosine_of_turns(coarse), cosine_of_turns(coarse + 0.25)
        for b in range(16):
            real, imag = coarse_real[b : b + 1], coarse_imag[b : b + 1]
            rows = pl.ds(b * 32, 32)
            near, far = pl.ds(2 * p * LANES, LANES), pl.ds((2 * p + 1) * LANES, LANES)
            y_table_ref[rows, near] = (real * fine_real - imag * fine_imag).astype(BF16)
            y_table_ref[rows, far] = (real * fine_imag + imag * fine_real).astype(BF16)
    for load in loads[2:]:
        load.wait()
    own_ref[:16] = measured[...]
    own_ref[16:, LANES // 2 :] = jnp.zeros((16, LANES // 2), F32)
    own_ref[16:, : LANES // 2] = weights[...]
    spectrum = dot(forward[...], columns[...], 1, 1)
    pairs = spectrum.shape[0] // 8
    near = spectrum[:, :LANES].reshape(pairs, 8, LANES)
    far = spectrum[:, LANES:].reshape(pairs, 8, LANES)
    low = iota(near.shape, 1) < 4
    even = jnp.where(low, near, pltpu.roll(far, 4, 1))
    odd = jnp.where(low, pltpu.roll(near, 4, 1), far)
    out_ref[...] = jnp.concatenate([even, odd], axis=1).reshape(out_ref.shape).astype(BF16)


def predict_kernel(scale, planes_ref, y_ref, x_ref, own_ref, out_ref):
    left = []
    for i in range(4):
        blocks = []
        for g in range(4):
            parts = [
                planes_ref[pl.ds(8 * peer, 8 * count), :] for peer, count in runs(OUT, zl=g, y=i)
            ]
            blocks.append(jnp.concatenate(parts, axis=0))
        left.append(jnp.concatenate(exchange_grains(blocks), axis=0))
    left = jnp.concatenate(left, axis=1)
    inner = dot(left, y_ref[...], 1, 0).astype(BF16)
    first = iota((8, LANES), 1) < LANES // 2
    for p in range(PLANES):
        near = inner[:, 2 * p * LANES : (2 * p + 1) * LANES]
        far = inner[:, (2 * p + 1) * LANES : (2 * p + 2) * LANES]
        points = dot(x_ref[p], jnp.concatenate([near, far], axis=0), 1, 0) * scale
        real, imag = points[:16], points[16:]
        out_ref[p, :8] = jnp.where(first, real[:8], pltpu.roll(imag[:8], 64, 1))
        out_ref[p, 8:16] = jnp.where(first, pltpu.roll(real[8:], 64, 1), imag[8:])
        out_ref[p, 16:] = jnp.zeros((16, LANES), F32)
    own = lax.axis_index("c")
    out_ref[own, :16] = out_ref[own, :16] - own_ref[:16]
    out_ref[own, 16:] = own_ref[16:]


def spread_kernel(scale, mine_ref, other_ref, y_ref, x_ref, misfit_ref, out_ref):
    first = iota((8, LANES), 1) < LANES // 2
    zero = jnp.zeros((8, LANES), F32)

    def both(weight):
        return jnp.where(first, weight, pltpu.roll(weight, 64, 1))

    def misfit_of(total):
        return total[:8] * both(total[16:24]), total[8:16] * both(total[24:])

    pieces = []
    for p in range(PLANES):
        near, far = misfit_of(mine_ref[p] + other_ref[p])
        spread = jnp.concatenate(
            [
                jnp.where(first, near, zero),
                jnp.where(first, zero, pltpu.roll(far, 64, 1)),
                jnp.where(first, pltpu.roll(near, 64, 1), zero),
                jnp.where(first, zero, far),
            ],
            axis=0,
        ).astype(BF16)
        inner = dot(x_ref[p], spread, 0, 0).astype(BF16)
        half = inner.shape[0] // 2
        pieces += [inner[:half], inner[half:]]
    planes = dot(jnp.concatenate(pieces, axis=1), y_ref[...], 1, 1) * scale
    planes = planes.astype(BF16)
    rows = planes.shape[0] // 4
    for i in range(4):
        lanes = slice(i * LANES, i * LANES + LANES)
        blocks = [planes[q * rows : q * rows + rows, lanes] for q in range(4)]
        blocks = exchange_grains(blocks)
        for g in range(4):
            row = 0
            for peer, count in runs(BACK, zl=g, y=i):
                part = blocks[g][row : row + 8 * count]
                out_ref[pl.ds(8 * peer, 8 * count), :] = part
                row += 8 * count
    own = lax.axis_index("c")
    near, far = misfit_of(mine_ref[own] + other_ref[own])
    misfit_ref[:8], misfit_ref[8:] = near, far


def update_kernel(planes_ref, columns_ref, table_ref, out_hbm, staged, sems):
    planes = planes_ref[...].astype(F32)
    planes = planes.reshape(planes.shape[0] // 16, 16, LANES)
    even, odd = planes[:, :8], planes[:, 8:]
    low = iota(even.shape, 1) < 4
    near = jnp.where(low, even, pltpu.roll(odd, 4, 1)).reshape(-1, LANES).astype(BF16)
    far = jnp.where(low, pltpu.roll(even, 4, 1), odd).reshape(-1, LANES).astype(BF16)
    table = table_ref[...]
    stores = []
    for i, back in enumerate((near, far)):
        part = pl.ds(i * LANES, LANES)
        correction = dot(back, table, 0, 0)
        staged[part, :] = (columns_ref[part, :].astype(F32) - 0.5 * correction).astype(BF16)
        stores.append(pltpu.make_async_copy(staged.at[part], out_hbm.at[part], sems.at[i]))
        stores[-1].start()
    for store in stores:
        store.wait()


VMEM = pl.BlockSpec(memory_space=pltpu.VMEM)
ANY = pl.BlockSpec(memory_space=pl.ANY)
HBM = pl.BlockSpec(memory_space=pltpu.HBM)


def pin(array):
    return pltpu.with_memory_space_constraint(array, pltpu.HBM)


def local_call(kernel, outs, operands, scratch=(), specs=None, out_specs=None, flops=2**27, limit=VMEM_LIMIT):
    return pl.pallas_call(
        kernel,
        out_shape=outs,
        in_specs=specs or [VMEM] * len(operands),
        out_specs=jax.tree.map(lambda _: VMEM, outs) if out_specs is None else out_specs,
        scratch_shapes=scratch,
        compiler_params=pltpu.CompilerParams(vmem_limit_bytes=limit),
        cost_estimate=pl.CostEstimate(flops=flops, bytes_accessed=flops // 128, transcendentals=0),
    )(*operands)


def shape_of(*shape, dtype=BF16):
    return jax.ShapeDtypeStruct(shape, dtype)


def exchange(array, peers):
    count = math.prod(AXES[a] for a in peers)
    blocks = array.reshape(count, array.shape[0] // count, array.shape[1])
    blocks = lax.all_to_all(blocks, peers, split_axis=0, concat_axis=0, tiled=True)
    return blocks.reshape(array.shape)


def shards(volume, x_frequency, y_frequency, measured, weights):
    x_local, y_local, length = volume.shape
    cells = x_local * y_local
    rows = cells * length // LANES
    planes, angles, kx_count = x_frequency.shape
    ky_count = y_frequency.shape[2]
    forward_scale = 1.0 / math.sqrt(cells * math.prod(AXES.values()))
    back_scale = 1.0 / math.sqrt(angles * kx_count * ky_count)
    columns = volume.reshape(cells, length)
    forward = column_table(length, 1.0 / math.sqrt(length), OUT)
    inverse = column_table(length, 1.0 / math.sqrt(planes), BACK)

    sending, own, x_table, y_table = local_call(
        start_kernel,
        (
            shape_of(rows, LANES),
            shape_of(32, LANES, dtype=F32),
            shape_of(PLANES, 32, 4 * LANES),
            shape_of(4 * LANES, 4 * LANES),
        ),
        (
            pin(x_frequency.transpose(1, 2, 0).reshape(angles * kx_count, planes)),
            pin(y_frequency.transpose(1, 2, 0).reshape(angles * ky_count, planes)),
            pin(columns),
            pin(jnp.asarray(forward)),
            pin(measured[0]),
            pin(weights[0]),
        ),
        [
            pltpu.VMEM((angles * kx_count, planes), jnp.int32),
            pltpu.VMEM((angles * ky_count, planes), jnp.int32),
            pltpu.VMEM((cells, length), BF16),
            pltpu.VMEM((length, length), BF16),
            pltpu.VMEM(measured.shape[1:], F32),
            pltpu.VMEM(weights.shape[1:], F32),
            pltpu.VMEM((planes, LANES), F32),
            pltpu.SemaphoreType.DMA((6,)),
        ],
        [HBM] * 6,
        limit=START_LIMIT,
    )
    received = exchange(sending, OUT)
    points = local_call(
        functools.partial(predict_kernel, forward_scale),
        shape_of(PLANES, 32, LANES, dtype=F32),
        (received, y_table, x_table, own),
    )
    others = lax.ppermute(points, "c", SWAP)
    misfit, sending = local_call(
        functools.partial(spread_kernel, back_scale),
        (shape_of(angles * kx_count, LANES, dtype=F32), shape_of(rows, LANES)),
        (points, others, y_table, x_table),
    )
    received = exchange(sending, BACK)
    updated = local_call(
        update_kernel,
        shape_of(cells, length),
        (received, columns, inverse),
        [pltpu.VMEM((cells, length), BF16), pltpu.SemaphoreType.DMA((2,))],
        out_specs=ANY,
    )
    return (updated.reshape(volume.shape), misfit.reshape(measured.shape))


def solution(mesh):
    fine = Mesh(mesh.devices.reshape(tuple(AXES.values())), tuple(AXES))
    placed = (
        P(ROWS, SLAB, None),
        P(),
        P(),
        P(SLAB + ROWS, None, None),
        P(SLAB + ROWS, None, None),
    )
    return jax.shard_map(
        shards,
        mesh=fine,
        in_specs=placed,
        out_specs=(P(ROWS, SLAB, None), P(SLAB + ROWS, None, None)),
        check_vma=False,
    )
```

```python
import functools
import math

import jax
import jax.numpy as jnp
import numpy as np
from jax import lax
from jax.experimental import pallas as pl
from jax.experimental.pallas import tpu as pltpu
from jax.sharding import Mesh
from jax.sharding import PartitionSpec as P

FINE = 4096
GRAIN = 32
LANES = 128
VMEM_LIMIT = 12 * 2**20
START_LIMIT = 12 * 2**20
F32 = jnp.float32
BF16 = jnp.bfloat16
AXES = {"y": 4, "zl": 4, "c": 2, "zh": 2, "x": 4}
SLAB = ("y", "zl", "c")
ROWS = ("zh", "x")
PEERS = ("zl", "y", "x", "zh")
PLANES = 2
SWAP = [(0, 1), (1, 0)]


def plane_of(**at):
    number = 0
    for axis in SLAB + ROWS:
        number = number * AXES[axis] + at[axis]
    return number


def column_table(length, scale):
    grid = np.arange(length // 2).reshape(4, 4, 2, 2, 2, 2)
    order = grid.transpose(1, 0, 4, 3, 5, 2).reshape(-1)
    depths = np.arange(length, dtype=np.int64)
    angles = (order[:, None] * depths[None, :] % length) * (2.0 * math.pi / length)
    matrix = np.stack([np.cos(angles), -np.sin(angles)], axis=1) * scale
    return matrix.reshape(length, length).astype(np.float32).astype(BF16)


def cosine_of_turns(turns):
    part = turns - jnp.floor(turns + 0.5)
    angle = (0.25 - jnp.abs(part)) * (2.0 * math.pi)
    square = angle * angle
    series = -1.0 / 39916800.0
    for term in (362880.0, -5040.0, 120.0, -6.0):
        series = series * square + 1.0 / term
    return angle + angle * square * series


def phases(turns):
    return cosine_of_turns(turns), cosine_of_turns(turns + 0.25)


def dot(left, right, left_dim, right_dim):
    dims = (((left_dim,), (right_dim,)), ((), ()))
    return lax.dot_general(left, right, dims, preferred_element_type=F32)


def iota(shape, axis):
    return lax.broadcasted_iota(jnp.int32, shape, axis)


def exchange_grains(blocks):
    lane = iota(blocks[0].shape, 1)
    low = lane < 2 * GRAIN
    even = (lane & GRAIN) == 0
    first = [None] * 4
    for i in (0, 1):
        a, b = blocks[i], blocks[i + 2]
        first[i] = jnp.where(low, a, pltpu.roll(b, 2 * GRAIN, 1))
        first[i + 2] = jnp.where(low, pltpu.roll(a, 2 * GRAIN, 1), b)
    last = [None] * 4
    for i in (0, 2):
        a, b = first[i], first[i + 1]
        last[i] = jnp.where(even, a, pltpu.roll(b, GRAIN, 1))
        last[i + 1] = jnp.where(even, pltpu.roll(a, 3 * GRAIN, 1), b)
    return last


def start_kernel(
    x_hbm,
    y_hbm,
    columns_hbm,
    forward_hbm,
    measured_hbm,
    weights_hbm,
    out_ref,
    own_ref,
    x_table_ref,
    y_table_ref,
    x_own,
    y_all,
    columns,
    forward,
    measured,
    weights,
    turned,
    sems,
):
    pairs = (
        (x_hbm, x_own),
        (y_hbm, y_all),
        (columns_hbm, columns),
        (forward_hbm, forward),
        (measured_hbm, measured),
        (weights_hbm, weights),
    )
    loads = [pltpu.make_async_copy(a, b, sems.at[i]) for i, (a, b) in enumerate(pairs)]
    for load in loads:
        load.start()
    at = {a: lax.axis_index(a) for a in SLAB + ROWS}
    lane = iota((16, 2 * LANES), 1)
    x_at = (lane >> 3 & 1) * 32 + (lane >> 4 & 3) * 8 + (lane >> 2 & 1) * 4 + (lane >> 6)
    x_at = x_at.astype(F32) * (1.0 / FINE)
    x_shift = (lane & 1).astype(F32) * 0.75
    team = lane >> 1 & 1
    y_in = iota((32, LANES), 0).astype(F32)
    y_block = (iota((16, LANES), 0) * 64 + at["c"] * 32).astype(F32)
    plane = [plane_of(**{**at, "c": p}) for p in range(PLANES)]
    for load in loads[:2]:
        load.wait()
    turned[...] = y_all[...].astype(F32).T
    x_all = x_own[...].astype(F32)
    lane_plane = iota(x_all.shape, 1)
    kx = [
        jnp.sum(jnp.where(lane_plane == k, x_all, 0.0), axis=1, keepdims=True) + FINE / 2.0
        for k in plane
    ]
    real, imag = phases(jnp.where(team == 0, kx[0], kx[1]) * x_at + x_shift)
    for p in range(PLANES):
        own_real = jnp.where(team == p, real, 0.0)
        own_imag = jnp.where(team == p, imag, 0.0)
        near, far = pl.ds(32 * p, 16), pl.ds(32 * p + 16, 16)
        x_table_ref[near, : 2 * LANES] = own_real.astype(BF16)
        x_table_ref[near, 2 * LANES :] = (-own_imag).astype(BF16)
        x_table_ref[far, : 2 * LANES] = own_imag.astype(BF16)
        x_table_ref[far, 2 * LANES :] = own_real.astype(BF16)
        ky = (turned[pl.ds(plane[p], 1), :] + FINE / 2.0) * (1.0 / FINE)
        fine = phases(ky * y_in)
        coarse = phases(ky * y_block)
        for b in range(16):
            real_b, imag_b = coarse[0][b : b + 1], coarse[1][b : b + 1]
            rows = pl.ds(b * 32, 32)
            near, far = pl.ds(p * LANES, LANES), pl.ds((PLANES + p) * LANES, LANES)
            y_table_ref[rows, near] = (real_b * fine[0] - imag_b * fine[1]).astype(BF16)
            y_table_ref[rows, far] = (real_b * fine[1] + imag_b * fine[0]).astype(BF16)
    for load in loads[2:]:
        load.wait()
    own_ref[:16] = measured[...]
    own_ref[16:, LANES // 2 :] = jnp.zeros((16, LANES // 2), F32)
    own_ref[16:, : LANES // 2] = weights[...]
    spectrum = dot(forward[...], columns[...], 1, 1).astype(BF16)
    near = spectrum[:, :LANES].reshape(-1, 16, LANES)
    far = spectrum[:, LANES:].reshape(-1, 16, LANES)
    even = (iota(near.shape, 1) & 4) == 0
    first = jnp.where(even, near, pltpu.roll(far, 4, 1))
    second = jnp.where(even, pltpu.roll(near, 12, 1), far)
    out_ref[...] = jnp.stack([first, second], axis=1).reshape(out_ref.shape)


def predict_kernel(scale, planes_ref, y_ref, x_ref, own_ref, out_ref):
    quarter = planes_ref.shape[0] // 4
    blocks = [planes_ref[pl.ds(g * quarter, quarter), :] for g in range(4)]
    blocks = exchange_grains(blocks)
    rows = quarter // 4
    left = [
        jnp.concatenate([b[i * rows : i * rows + rows] for b in blocks], axis=0)
        for i in range(4)
    ]
    inner = dot(jnp.concatenate(left, axis=1), y_ref[...], 1, 0).astype(BF16)
    inner = jnp.concatenate([inner[:, : 2 * LANES], inner[:, 2 * LANES :]], axis=0)
    both = dot(x_ref[...], inner, 1, 0)
    first = iota((8, LANES), 1) < LANES // 2
    for p in range(PLANES):
        points = both[32 * p : 32 * p + 32, LANES * p : LANES * p + LANES] * scale
        real, imag = points[:16], points[16:]
        out_ref[p, :8] = jnp.where(first, real[:8], pltpu.roll(imag[:8], 64, 1))
        out_ref[p, 8:16] = jnp.where(first, pltpu.roll(real[8:], 64, 1), imag[8:])
        out_ref[p, 16:] = jnp.zeros((16, LANES), F32)
    own = lax.axis_index("c")
    out_ref[own, :16] = out_ref[own, :16] - own_ref[:16]
    out_ref[own, 16:] = own_ref[16:]


def spread_kernel(scale, mine_ref, other_ref, y_ref, x_ref, misfit_ref, out_ref):
    first = iota((8, LANES), 1) < LANES // 2
    zero = jnp.zeros((8, LANES), F32)

    def both(weight):
        return jnp.where(first, weight, pltpu.roll(weight, 64, 1))

    def misfit_of(total):
        return total[:8] * both(total[16:24]), total[8:16] * both(total[24:])

    lanes = []
    for p in range(PLANES):
        near, far = misfit_of(mine_ref[p] + other_ref[p])
        near, far = near * scale, far * scale
        spread = [
            jnp.where(first, near, zero),
            jnp.where(first, zero, pltpu.roll(far, 64, 1)),
            jnp.where(first, pltpu.roll(near, 64, 1), zero),
            jnp.where(first, zero, far),
        ]
        lanes.append(jnp.concatenate([zero] * 4 * p + spread + [zero] * 4 * (1 - p), axis=0))
    inner = dot(x_ref[...], jnp.concatenate(lanes, axis=1).astype(BF16), 0, 0).astype(BF16)
    inner = jnp.concatenate([inner[: 2 * LANES], inner[2 * LANES :]], axis=1)
    planes = dot(inner, y_ref[...], 1, 1).astype(BF16)
    rows = planes.shape[0] // 4
    for i in range(4):
        lanes = slice(i * LANES, i * LANES + LANES)
        blocks = [planes[q * rows : q * rows + rows, lanes] for q in range(4)]
        blocks = exchange_grains(blocks)
        for g in range(4):
            out_ref[pl.ds((4 * g + i) * rows, rows), :] = blocks[g]
    own = lax.axis_index("c")
    near, far = misfit_of(mine_ref[own] + other_ref[own])
    misfit_ref[:8], misfit_ref[8:] = near, far


def update_kernel(planes_ref, columns_ref, table_ref, out_hbm, staged, sems):
    planes = planes_ref[...].reshape(-1, 2, 16, LANES)
    first, second = planes[:, 0], planes[:, 1]
    even = (iota(first.shape, 1) & 4) == 0
    near = jnp.where(even, first, pltpu.roll(second, 4, 1)).reshape(-1, LANES)
    far = jnp.where(even, pltpu.roll(first, 12, 1), second).reshape(-1, LANES)
    table = table_ref[...]
    stores = []
    for i, back in enumerate((near, far)):
        part = pl.ds(i * LANES, LANES)
        correction = dot(back, table, 0, 0)
        staged[part, :] = (columns_ref[part, :].astype(F32) - 0.5 * correction).astype(BF16)
        stores.append(pltpu.make_async_copy(staged.at[part], out_hbm.at[part], sems.at[i]))
        stores[-1].start()
    for store in stores:
        store.wait()


VMEM = pl.BlockSpec(memory_space=pltpu.VMEM)
ANY = pl.BlockSpec(memory_space=pl.ANY)
HBM = pl.BlockSpec(memory_space=pltpu.HBM)


def pin(array):
    return pltpu.with_memory_space_constraint(array, pltpu.HBM)


def local_call(kernel, outs, operands, scratch=(), specs=None, out_specs=None, flops=2**27, limit=VMEM_LIMIT):
    return pl.pallas_call(
        kernel,
        out_shape=outs,
        in_specs=specs or [VMEM] * len(operands),
        out_specs=jax.tree.map(lambda _: VMEM, outs) if out_specs is None else out_specs,
        scratch_shapes=scratch,
        compiler_params=pltpu.CompilerParams(vmem_limit_bytes=limit),
        cost_estimate=pl.CostEstimate(flops=flops, bytes_accessed=flops // 128, transcendentals=0),
    )(*operands)


def shape_of(*shape, dtype=BF16):
    return jax.ShapeDtypeStruct(shape, dtype)


def exchange(array):
    count = math.prod(AXES[a] for a in PEERS)
    blocks = array.reshape(count, array.shape[0] // count, array.shape[1])
    blocks = lax.all_to_all(blocks, PEERS, split_axis=0, concat_axis=0, tiled=True)
    return blocks.reshape(array.shape)


def shards(volume, x_frequency, y_frequency, measured, weights):
    x_local, y_local, length = volume.shape
    cells = x_local * y_local
    rows = cells * length // LANES
    planes, angles, kx_count = x_frequency.shape
    ky_count = y_frequency.shape[2]
    forward_scale = 1.0 / math.sqrt(cells * math.prod(AXES.values()))
    back_scale = 1.0 / math.sqrt(angles * kx_count * ky_count)
    columns = volume.reshape(cells, length)
    forward = column_table(length, 1.0 / math.sqrt(length))
    inverse = column_table(length, 1.0 / math.sqrt(planes))

    sending, own, x_table, y_table = local_call(
        start_kernel,
        (
            shape_of(rows, LANES),
            shape_of(32, LANES, dtype=F32),
            shape_of(PLANES * 32, 4 * LANES),
            shape_of(4 * LANES, 4 * LANES),
        ),
        (
            pin(x_frequency.transpose(1, 2, 0).reshape(angles * kx_count, planes)),
            pin(y_frequency.transpose(1, 2, 0).reshape(angles * ky_count, planes)),
            pin(columns),
            pin(jnp.asarray(forward)),
            pin(measured[0]),
            pin(weights[0]),
        ),
        [
            pltpu.VMEM((angles * kx_count, planes), jnp.int32),
            pltpu.VMEM((angles * ky_count, planes), jnp.int32),
            pltpu.VMEM((cells, length), BF16),
            pltpu.VMEM((length, length), BF16),
            pltpu.VMEM(measured.shape[1:], F32),
            pltpu.VMEM(weights.shape[1:], F32),
            pltpu.VMEM((planes, LANES), F32),
            pltpu.SemaphoreType.DMA((6,)),
        ],
        [HBM] * 6,
        limit=START_LIMIT,
    )
    received = exchange(sending)
    points = local_call(
        functools.partial(predict_kernel, forward_scale),
        shape_of(PLANES, 32, LANES, dtype=F32),
        (received, y_table, x_table, own),
    )
    others = lax.ppermute(points, "c", SWAP)
    misfit, sending = local_call(
        functools.partial(spread_kernel, back_scale),
        (shape_of(angles * kx_count, LANES, dtype=F32), shape_of(rows, LANES)),
        (points, others, y_table, x_table),
    )
    received = exchange(sending)
    updated = local_call(
        update_kernel,
        shape_of(cells, length),
        (received, columns, inverse),
        [pltpu.VMEM((cells, length), BF16), pltpu.SemaphoreType.DMA((2,))],
        out_specs=ANY,
    )
    return (updated.reshape(volume.shape), misfit.reshape(measured.shape))


def solution(mesh):
    fine = Mesh(mesh.devices.reshape(tuple(AXES.values())), tuple(AXES))
    placed = (
        P(ROWS, SLAB, None),
        P(),
        P(),
        P(SLAB + ROWS, None, None),
        P(SLAB + ROWS, None, None),
    )
    return jax.shard_map(
        shards,
        mesh=fine,
        in_specs=placed,
        out_specs=(P(ROWS, SLAB, None), P(SLAB + ROWS, None, None)),
        check_vma=False,
    )
```

```python
import functools
import math

import jax
import jax.numpy as jnp
import numpy as np
from jax import lax
from jax.experimental import pallas as pl
from jax.experimental.pallas import tpu as pltpu
from jax.sharding import Mesh
from jax.sharding import PartitionSpec as P

FINE = 4096
LANES = 128
VMEM_LIMIT = 12 * 2**20
F32 = jnp.float32
BF16 = jnp.bfloat16
AXES = {"yh": 2, "yl": 2, "zl": 4, "c": 2, "zh": 2, "x": 4}
SLAB = ("yh", "yl", "zl", "c")
ROWS = ("zh", "x")
PEERS = ("zl", "yl", "zh", "x")
TEAM = ("yh", "c")
PLANES = 4
SWAP = [(0, 1), (1, 0)]


def plane_of(at):
    number = 0
    for axis in SLAB + ROWS:
        number = number * AXES[axis] + at[axis]
    return number


def column_table(length, scale):
    grid = np.arange(length // 2).reshape([AXES[a] for a in SLAB + ROWS])
    order = grid.transpose([(SLAB + ROWS).index(a) for a in PEERS + TEAM]).reshape(-1)
    depths = np.arange(length, dtype=np.int64)
    angles = (order[:, None] * depths[None, :] % length) * (2.0 * math.pi / length)
    matrix = np.stack([np.cos(angles), -np.sin(angles)], axis=1) * scale
    return matrix.reshape(length, length).astype(np.float32).astype(BF16)


def cosine_of_turns(turns):
    part = turns - jnp.floor(turns + 0.5)
    angle = (0.25 - jnp.abs(part)) * (2.0 * math.pi)
    square = angle * angle
    series = -1.0 / 39916800.0
    for term in (362880.0, -5040.0, 120.0, -6.0):
        series = series * square + 1.0 / term
    return angle + angle * square * series


def phases(turns):
    return cosine_of_turns(turns), cosine_of_turns(turns + 0.25)


def product(left, right):
    return (
        left[0] * right[0] - left[1] * right[1],
        left[0] * right[1] + left[1] * right[0],
    )


def dot(left, right, left_dim, right_dim):
    dims = (((left_dim,), (right_dim,)), ((), ()))
    return lax.dot_general(left, right, dims, preferred_element_type=F32)


def iota(shape, axis):
    return lax.broadcasted_iota(jnp.int32, shape, axis)


def exchange_grains(blocks, axis, grain):
    size = blocks[0].shape[axis]
    place = iota(blocks[0].shape, axis) & (4 * grain - 1)
    low = place < 2 * grain
    even = (place & grain) == 0
    first = [None] * 4
    for i in (0, 1):
        a, b = blocks[i], blocks[i + 2]
        first[i] = jnp.where(low, a, pltpu.roll(b, 2 * grain, axis))
        first[i + 2] = jnp.where(low, pltpu.roll(a, size - 2 * grain, axis), b)
    last = [None] * 4
    for i in (0, 2):
        a, b = first[i], first[i + 1]
        last[i] = jnp.where(even, a, pltpu.roll(b, grain, axis))
        last[i + 1] = jnp.where(even, pltpu.roll(a, size - grain, axis), b)
    return last


def start_kernel(
    x_hbm,
    y_hbm,
    columns_hbm,
    forward_hbm,
    measured_hbm,
    weights_hbm,
    out_ref,
    own_ref,
    x_table_ref,
    y_table_ref,
    x_all,
    y_all,
    columns,
    forward,
    measured,
    weights,
    turned,
    sems,
):
    pairs = (
        (x_hbm, x_all),
        (y_hbm, y_all),
        (columns_hbm, columns),
        (forward_hbm, forward),
        (measured_hbm, measured),
        (weights_hbm, weights),
    )
    loads = [pltpu.make_async_copy(a, b, sems.at[i]) for i, (a, b) in enumerate(pairs)]
    for load in loads:
        load.start()
    at = {a: lax.axis_index(a) for a in SLAB + ROWS}
    lane = iota((16, LANES), 1)
    x_at = (lane >> 4 & 1) * 32 + (lane >> 1 & 3) * 8 + (lane >> 3 & 1) * 4 + (lane >> 5)
    x_at = x_at.astype(F32) * (1.0 / FINE)
    x_shift = (lane & 1).astype(F32) * 0.75
    y_in = iota((32, LANES), 0).astype(F32)
    block = iota((8, LANES), 0)
    y_block = (block * 64 + at["yh"] * 512 + at["c"] * 32).astype(F32)
    plane = [plane_of({**at, "yh": p >> 1, "c": p & 1}) for p in range(PLANES)]
    for load in loads[:2]:
        load.wait()
    turned[...] = y_all[...].astype(F32).T
    x_own = x_all[...].astype(F32)
    lane_plane = iota(x_own.shape, 1)
    for p in range(PLANES):
        ky = (turned[pl.ds(plane[p], 1), :] + FINE / 2.0) * (1.0 / FINE)
        fine = phases(ky * y_in)
        coarse = phases(ky * y_block)
        for b in range(8):
            real, imag = product((coarse[0][b : b + 1], coarse[1][b : b + 1]), fine)
            y_table_ref[p, pl.ds(b * 32, 32), :LANES] = real.astype(BF16)
            y_table_ref[p, pl.ds(b * 32, 32), LANES:] = imag.astype(BF16)
        kx = jnp.sum(jnp.where(lane_plane == plane[p], x_own, 0.0), axis=1, keepdims=True)
        real, imag = phases((kx + FINE / 2.0) * x_at + x_shift)
        real, imag, back = real.astype(BF16), imag.astype(BF16), (-imag).astype(BF16)
        x_table_ref[pl.ds(32 * p, 16), :LANES] = real
        x_table_ref[pl.ds(32 * p, 16), LANES:] = back
        x_table_ref[pl.ds(32 * p + 16, 16), :LANES] = imag
        x_table_ref[pl.ds(32 * p + 16, 16), LANES:] = real
    for load in loads[2:]:
        load.wait()
    own_ref[:16] = measured[...]
    own_ref[16:, : LANES // 2] = weights[:8]
    own_ref[16:, LANES // 2 :] = weights[8:]
    spectrum = dot(forward[...], columns[...], 1, 1)
    near = spectrum[:, :LANES].reshape(-1, 8, LANES)
    far = spectrum[:, LANES:].reshape(-1, 8, LANES)
    out_ref[...] = jnp.concatenate([near, far], axis=1).reshape(out_ref.shape).astype(BF16)


def own_plane():
    return lax.axis_index("yh") * 2 + lax.axis_index("c")


def predict_kernel(scale, planes_ref, y_ref, x_ref, own_ref, out_ref):
    quarter = planes_ref.shape[0] // 4
    blocks = [planes_ref[pl.ds(g * quarter, quarter), :] for g in range(4)]
    blocks = exchange_grains(blocks, 1, 32)
    left = [[[], []] for _ in range(PLANES)]
    for q in range(4):
        rows = blocks[q].reshape(2, 2, 4, 16, LANES)
        for i in range(2):
            parts = exchange_grains([rows[i, :, x] for x in range(4)], 1, 2)
            for p in range(PLANES):
                left[p][i].append(parts[p].reshape(-1, LANES))
    near, far = [], []
    for p in range(PLANES):
        side = jnp.concatenate([jnp.concatenate(half, axis=0) for half in left[p]], axis=1)
        inner = dot(side, y_ref[p], 1, 0).astype(BF16)
        near.append(inner[:, :LANES])
        far.append(inner[:, LANES:])
    inner = jnp.concatenate(
        [jnp.concatenate(near, axis=1), jnp.concatenate(far, axis=1)], axis=0
    )
    everything = dot(x_ref[...], inner, 1, 0)
    first = iota((8, LANES), 1) < LANES // 2
    for p in range(PLANES):
        points = everything[32 * p : 32 * p + 32, LANES * p : LANES * p + LANES] * scale
        real, imag = points[:16], points[16:]
        out_ref[p, :8] = jnp.where(first, real[:8], pltpu.roll(imag[:8], 64, 1))
        out_ref[p, 8:16] = jnp.where(first, pltpu.roll(real[8:], 64, 1), imag[8:])
        out_ref[p, 16:] = jnp.zeros((8, LANES), F32)
    own = own_plane()
    out_ref[own, :16] = out_ref[own, :16] - own_ref[:16]
    out_ref[own, 16:] = own_ref[16:]


def spread_kernel(scale, sum_ref, other_ref, y_ref, x_ref, misfit_ref, out_ref):
    first = iota((8, LANES), 1) < LANES // 2

    def misfit_of(total):
        near, far, weight = total[:8], total[8:16], total[16:]
        crossed = pltpu.roll(weight, 64, 1)
        return (
            near * jnp.where(first, weight, crossed),
            far * jnp.where(first, crossed, weight),
        )

    zero = jnp.zeros((8, LANES), F32)
    lanes = []
    for p in range(PLANES):
        near, far = misfit_of(sum_ref[p] + other_ref[p].astype(F32))
        near, far = near * scale, far * scale
        spread = [
            jnp.where(first, near, zero),
            jnp.where(first, zero, pltpu.roll(far, 64, 1)),
            jnp.where(first, pltpu.roll(near, 64, 1), zero),
            jnp.where(first, zero, far),
        ]
        before, after = [zero] * 4 * p, [zero] * 4 * (PLANES - 1 - p)
        lanes.append(jnp.concatenate(before + spread + after, axis=0))
    everything = dot(x_ref[...], jnp.concatenate(lanes, axis=1).astype(BF16), 0, 0).astype(BF16)
    planes = []
    for p in range(PLANES):
        inner = everything[:, LANES * p : LANES * p + LANES]
        inner = jnp.concatenate([inner[:LANES], inner[LANES:]], axis=1)
        plane = dot(inner, y_ref[p], 1, 1).astype(BF16)
        planes.append(plane.reshape(4, 2, 16, 2 * LANES))
    blocks = []
    for q in range(4):
        rows = []
        for i in range(2):
            part = slice(i * LANES, i * LANES + LANES)
            parts = exchange_grains([planes[p][q, :, :, part] for p in range(PLANES)], 1, 2)
            rows.append(jnp.stack(parts, axis=1).reshape(-1, LANES))
        blocks.append(jnp.concatenate(rows, axis=0))
    blocks = exchange_grains(blocks, 1, 32)
    quarter = out_ref.shape[0] // 4
    for g in range(4):
        out_ref[pl.ds(g * quarter, quarter), :] = blocks[g]
    own = own_plane()
    near, far = misfit_of(sum_ref[own] + other_ref[own].astype(F32))
    misfit_ref[:8], misfit_ref[8:] = near, far


def update_kernel(planes_ref, columns_ref, table_ref, out_hbm, staged, sems):
    planes = planes_ref[...].astype(F32).reshape(-1, 2, 8, LANES)
    table = table_ref[...]
    stores = []
    for i in range(2):
        part = pl.ds(i * LANES, LANES)
        correction = dot(planes[:, i].reshape(-1, LANES).astype(BF16), table, 0, 0)
        staged[part, :] = (columns_ref[part, :].astype(F32) - 0.5 * correction).astype(BF16)
        stores.append(pltpu.make_async_copy(staged.at[part], out_hbm.at[part], sems.at[i]))
        stores[-1].start()
    for store in stores:
        store.wait()


VMEM = pl.BlockSpec(memory_space=pltpu.VMEM)
HBM = pl.BlockSpec(memory_space=pltpu.HBM)
ANY = pl.BlockSpec(memory_space=pl.ANY)


def pin(array):
    return pltpu.with_memory_space_constraint(array, pltpu.HBM)


def local_call(kernel, outs, operands, scratch=(), specs=None, out_specs=None):
    return pl.pallas_call(
        kernel,
        out_shape=outs,
        in_specs=specs or [VMEM] * len(operands),
        out_specs=jax.tree.map(lambda _: VMEM, outs) if out_specs is None else out_specs,
        scratch_shapes=scratch,
        compiler_params=pltpu.CompilerParams(vmem_limit_bytes=VMEM_LIMIT),
        cost_estimate=pl.CostEstimate(flops=2**27, bytes_accessed=2**20, transcendentals=0),
    )(*operands)


def shape_of(*shape, dtype=BF16):
    return jax.ShapeDtypeStruct(shape, dtype)


def exchange(array):
    count = math.prod(AXES[a] for a in PEERS)
    blocks = array.reshape(count, array.shape[0] // count, array.shape[1])
    blocks = lax.all_to_all(blocks, PEERS, split_axis=0, concat_axis=0, tiled=True)
    return blocks.reshape(array.shape)


def shards(volume, x_frequency, y_frequency, measured, weights):
    x_local, y_local, length = volume.shape
    cells = x_local * y_local
    rows = cells * length // LANES
    planes, angles, kx_count = x_frequency.shape
    ky_count = y_frequency.shape[2]
    forward_scale = 1.0 / math.sqrt(cells * math.prod(AXES.values()))
    back_scale = 1.0 / math.sqrt(angles * kx_count * ky_count)
    columns = volume.reshape(cells, length)
    forward = column_table(length, 1.0 / math.sqrt(length))
    inverse = column_table(length, 1.0 / math.sqrt(planes))

    sending, own, x_table, y_table = local_call(
        start_kernel,
        (
            shape_of(rows, LANES),
            shape_of(24, LANES, dtype=F32),
            shape_of(PLANES * 32, 2 * LANES),
            shape_of(PLANES, 2 * LANES, 2 * LANES),
        ),
        (
            pin(x_frequency.transpose(1, 2, 0).reshape(angles * kx_count, planes)),
            pin(y_frequency.transpose(1, 2, 0).reshape(angles * ky_count, planes)),
            pin(columns),
            pin(jnp.asarray(forward)),
            pin(measured[0]),
            pin(weights[0]),
        ),
        [
            pltpu.VMEM((angles * kx_count, planes), jnp.int32),
            pltpu.VMEM((angles * ky_count, planes), jnp.int32),
            pltpu.VMEM((cells, length), BF16),
            pltpu.VMEM((length, length), BF16),
            pltpu.VMEM(measured.shape[1:], F32),
            pltpu.VMEM(weights.shape[1:], F32),
            pltpu.VMEM((planes, LANES), F32),
            pltpu.SemaphoreType.DMA((6,)),
        ],
        [HBM] * 6,
    )
    received = exchange(sending)
    total = local_call(
        functools.partial(predict_kernel, forward_scale),
        shape_of(PLANES, 24, LANES, dtype=F32),
        (received, y_table, x_table, own),
    )
    total = total + lax.ppermute(total, "c", SWAP)
    other = lax.ppermute(total.astype(BF16), "yh", SWAP)
    misfit, sending = local_call(
        functools.partial(spread_kernel, back_scale),
        (shape_of(angles * kx_count, LANES, dtype=F32), shape_of(rows, LANES)),
        (total, other, y_table, x_table),
    )
    received = exchange(sending)
    updated = local_call(
        update_kernel,
        shape_of(cells, length),
        (received, columns, inverse),
        [pltpu.VMEM((cells, length), BF16), pltpu.SemaphoreType.DMA((2,))],
        out_specs=ANY,
    )
    return (updated.reshape(volume.shape), misfit.reshape(measured.shape))


def solution(mesh):
    fine = Mesh(mesh.devices.reshape(tuple(AXES.values())), tuple(AXES))
    placed = (
        P(ROWS, SLAB, None),
        P(),
        P(),
        P(SLAB + ROWS, None, None),
        P(SLAB + ROWS, None, None),
    )
    return jax.shard_map(
        shards,
        mesh=fine,
        in_specs=placed,
        out_specs=(P(ROWS, SLAB, None), P(SLAB + ROWS, None, None)),
        check_vma=False,
    )
```

```python
import functools
import math

import jax
import jax.numpy as jnp
import numpy as np
from jax import lax
from jax.experimental import pallas as pl
from jax.experimental.pallas import tpu as pltpu
from jax.sharding import Mesh
from jax.sharding import PartitionSpec as P

FINE = 4096
LANES = 128
VMEM_LIMIT = 12 * 2**20
F32 = jnp.float32
BF16 = jnp.bfloat16
AXES = {"yh": 2, "yl": 2, "zl": 4, "c": 2, "zh": 2, "x": 4}
SLAB = ("yh", "yl", "zl", "c")
ROWS = ("zh", "x")
PEERS = ("zl", "zh", "x", "yl")
TEAM = ("yh", "c")
PLANES = 4
SWAP = [(0, 1), (1, 0)]


def plane_of(at):
    number = 0
    for axis in SLAB + ROWS:
        number = number * AXES[axis] + at[axis]
    return number


def column_table(length, scale):
    grid = np.arange(length // 2).reshape([AXES[a] for a in SLAB + ROWS])
    order = grid.transpose([(SLAB + ROWS).index(a) for a in PEERS + TEAM]).reshape(-1)
    depths = np.arange(length, dtype=np.int64)
    angles = (order[:, None] * depths[None, :] % length) * (2.0 * math.pi / length)
    matrix = np.stack([np.cos(angles), -np.sin(angles)], axis=1) * scale
    return matrix.reshape(length, length).astype(np.float32).astype(BF16)


def cosine_of_turns(turns):
    part = turns - jnp.floor(turns + 0.5)
    angle = (0.25 - jnp.abs(part)) * (2.0 * math.pi)
    square = angle * angle
    series = -1.0 / 39916800.0
    for term in (362880.0, -5040.0, 120.0, -6.0):
        series = series * square + 1.0 / term
    return angle + angle * square * series


def phases(turns):
    return cosine_of_turns(turns), cosine_of_turns(turns + 0.25)


def product(left, right):
    return (
        left[0] * right[0] - left[1] * right[1],
        left[0] * right[1] + left[1] * right[0],
    )


def dot(left, right, left_dim, right_dim):
    dims = (((left_dim,), (right_dim,)), ((), ()))
    return lax.dot_general(left, right, dims, preferred_element_type=F32)


def iota(shape, axis):
    return lax.broadcasted_iota(jnp.int32, shape, axis)


def exchange_grains(blocks, axis, grain):
    size = blocks[0].shape[axis]
    place = iota(blocks[0].shape, axis) & (4 * grain - 1)
    low = place < 2 * grain
    even = (place & grain) == 0
    first = [None] * 4
    for i in (0, 1):
        a, b = blocks[i], blocks[i + 2]
        first[i] = jnp.where(low, a, pltpu.roll(b, 2 * grain, axis))
        first[i + 2] = jnp.where(low, pltpu.roll(a, size - 2 * grain, axis), b)
    last = [None] * 4
    for i in (0, 2):
        a, b = first[i], first[i + 1]
        last[i] = jnp.where(even, a, pltpu.roll(b, grain, axis))
        last[i + 1] = jnp.where(even, pltpu.roll(a, size - grain, axis), b)
    return last


def start_kernel(
    x_hbm,
    y_hbm,
    columns_hbm,
    forward_hbm,
    measured_hbm,
    weights_hbm,
    out_ref,
    own_ref,
    x_table_ref,
    y_table_ref,
    x_all,
    y_all,
    columns,
    forward,
    measured,
    weights,
    turned,
    sems,
):
    pairs = (
        (x_hbm, x_all),
        (y_hbm, y_all),
        (columns_hbm, columns),
        (forward_hbm, forward),
        (measured_hbm, measured),
        (weights_hbm, weights),
    )
    loads = [pltpu.make_async_copy(a, b, sems.at[i]) for i, (a, b) in enumerate(pairs)]
    for load in loads:
        load.start()
    at = {a: lax.axis_index(a) for a in SLAB + ROWS}
    lane = iota((16, LANES), 1)
    x_at = (lane >> 4 & 1) * 32 + (lane >> 1 & 3) * 8 + (lane >> 3 & 1) * 4 + (lane >> 5)
    x_at = x_at.astype(F32) * (1.0 / FINE)
    x_shift = (lane & 1).astype(F32) * 0.75
    row = iota((8, LANES), 0)
    y_in = row.astype(F32)
    y_middle = (row * 8).astype(F32)
    y_block = (row * 64 + at["yh"] * 512 + at["c"] * 32).astype(F32)
    plane = [plane_of({**at, "yh": p >> 1, "c": p & 1}) for p in range(PLANES)]
    for load in loads[:2]:
        load.wait()
    turned[...] = y_all[...].astype(F32).T
    x_own = x_all[...].astype(F32)
    lane_plane = iota(x_own.shape, 1)
    for p in range(PLANES):
        ky = (turned[pl.ds(plane[p], 1), :] + FINE / 2.0) * (1.0 / FINE)
        fine = phases(ky * y_in)
        middle = phases(ky * y_middle)
        coarse = phases(ky * y_block)
        inner = [product((middle[0][b : b + 1], middle[1][b : b + 1]), fine) for b in range(4)]
        inner = [jnp.concatenate([m[i] for m in inner], axis=0) for i in range(2)]
        for b in range(8):
            real, imag = product((coarse[0][b : b + 1], coarse[1][b : b + 1]), inner)
            y_table_ref[p, pl.ds(b * 32, 32), :LANES] = real.astype(BF16)
            y_table_ref[p, pl.ds(b * 32, 32), LANES:] = imag.astype(BF16)
        kx = jnp.sum(jnp.where(lane_plane == plane[p], x_own, 0.0), axis=1, keepdims=True)
        real, imag = phases((kx + FINE / 2.0) * x_at + x_shift)
        real, imag, back = real.astype(BF16), imag.astype(BF16), (-imag).astype(BF16)
        x_table_ref[pl.ds(32 * p, 16), :LANES] = real
        x_table_ref[pl.ds(32 * p, 16), LANES:] = back
        x_table_ref[pl.ds(32 * p + 16, 16), :LANES] = imag
        x_table_ref[pl.ds(32 * p + 16, 16), LANES:] = real
    for load in loads[2:]:
        load.wait()
    own_ref[:16] = measured[...]
    own_ref[16:, : LANES // 2] = weights[:8]
    own_ref[16:, LANES // 2 :] = weights[8:]
    spectrum = dot(forward[...], columns[...], 1, 1)
    near = spectrum[:, :LANES].reshape(-1, 8, LANES)
    far = spectrum[:, LANES:].reshape(-1, 8, LANES)
    out_ref[...] = jnp.concatenate([near, far], axis=1).reshape(out_ref.shape).astype(BF16)


def own_plane():
    return lax.axis_index("yh") * 2 + lax.axis_index("c")


def predict_kernel(scale, planes_ref, y_ref, x_ref, own_ref, out_ref):
    quarter = planes_ref.shape[0] // 4
    blocks = [planes_ref[pl.ds(g * quarter, quarter), :] for g in range(4)]
    blocks = exchange_grains(blocks, 1, 32)
    left = [[[], []] for _ in range(PLANES)]
    for q in range(4):
        rows = blocks[q].reshape(2, 4, 2, 16, LANES)
        for i in range(2):
            parts = exchange_grains([rows[:, x, i] for x in range(4)], 1, 2)
            for p in range(PLANES):
                left[p][i].append(parts[p].reshape(-1, LANES))
    near, far = [], []
    for p in range(PLANES):
        side = jnp.concatenate([jnp.concatenate(half, axis=0) for half in left[p]], axis=1)
        inner = dot(side, y_ref[p], 1, 0).astype(BF16)
        near.append(inner[:, :LANES])
        far.append(inner[:, LANES:])
    inner = jnp.concatenate(
        [jnp.concatenate(near, axis=1), jnp.concatenate(far, axis=1)], axis=0
    )
    everything = dot(x_ref[...], inner, 1, 0)
    first = iota((8, LANES), 1) < LANES // 2
    for p in range(PLANES):
        points = everything[32 * p : 32 * p + 32, LANES * p : LANES * p + LANES] * scale
        real, imag = points[:16], points[16:]
        out_ref[p, :8] = jnp.where(first, real[:8], pltpu.roll(imag[:8], 64, 1))
        out_ref[p, 8:16] = jnp.where(first, pltpu.roll(real[8:], 64, 1), imag[8:])
        out_ref[p, 16:] = jnp.zeros((8, LANES), F32)
    own = own_plane()
    out_ref[own, :16] = out_ref[own, :16] - own_ref[:16]
    out_ref[own, 16:] = own_ref[16:]


def spread_kernel(scale, sum_ref, other_ref, y_ref, x_ref, misfit_ref, out_ref):
    first = iota((8, LANES), 1) < LANES // 2

    def misfit_of(total):
        near, far, weight = total[:8], total[8:16], total[16:]
        crossed = pltpu.roll(weight, 64, 1)
        return (
            near * jnp.where(first, weight, crossed),
            far * jnp.where(first, crossed, weight),
        )

    zero = jnp.zeros((8, LANES), F32)
    lanes = []
    for p in range(PLANES):
        near, far = misfit_of(sum_ref[p] + other_ref[p].astype(F32))
        near, far = near * scale, far * scale
        spread = [
            jnp.where(first, near, zero),
            jnp.where(first, zero, pltpu.roll(far, 64, 1)),
            jnp.where(first, pltpu.roll(near, 64, 1), zero),
            jnp.where(first, zero, far),
        ]
        before, after = [zero] * 4 * p, [zero] * 4 * (PLANES - 1 - p)
        lanes.append(jnp.concatenate(before + spread + after, axis=0))
    everything = dot(x_ref[...], jnp.concatenate(lanes, axis=1).astype(BF16), 0, 0).astype(BF16)
    planes = []
    for p in range(PLANES):
        inner = everything[:, LANES * p : LANES * p + LANES]
        inner = jnp.concatenate([inner[:LANES], inner[LANES:]], axis=1)
        plane = dot(inner, y_ref[p], 1, 1).astype(BF16)
        planes.append(plane.reshape(4, 2, 16, 2 * LANES))
    blocks = []
    for q in range(4):
        rows = []
        for i in range(2):
            part = slice(i * LANES, i * LANES + LANES)
            parts = exchange_grains([planes[p][q, :, :, part] for p in range(PLANES)], 1, 2)
            rows.append(jnp.stack(parts, axis=1))
        blocks.append(jnp.stack(rows, axis=2).reshape(-1, LANES))
    blocks = exchange_grains(blocks, 1, 32)
    quarter = out_ref.shape[0] // 4
    for g in range(4):
        out_ref[pl.ds(g * quarter, quarter), :] = blocks[g]
    own = own_plane()
    near, far = misfit_of(sum_ref[own] + other_ref[own].astype(F32))
    misfit_ref[:8], misfit_ref[8:] = near, far


def update_kernel(planes_ref, columns_ref, table_ref, out_hbm, staged, sems):
    planes = planes_ref[...].astype(F32).reshape(-1, 2, 8, LANES)
    table = table_ref[...]
    stores = []
    for i in range(2):
        part = pl.ds(i * LANES, LANES)
        correction = dot(planes[:, i].reshape(-1, LANES).astype(BF16), table, 0, 0)
        staged[part, :] = (columns_ref[part, :].astype(F32) - 0.5 * correction).astype(BF16)
        stores.append(pltpu.make_async_copy(staged.at[part], out_hbm.at[part], sems.at[i]))
        stores[-1].start()
    for store in stores:
        store.wait()


VMEM = pl.BlockSpec(memory_space=pltpu.VMEM)
HBM = pl.BlockSpec(memory_space=pltpu.HBM)
ANY = pl.BlockSpec(memory_space=pl.ANY)


def pin(array):
    return pltpu.with_memory_space_constraint(array, pltpu.HBM)


def local_call(kernel, outs, operands, scratch=(), specs=None, out_specs=None):
    return pl.pallas_call(
        kernel,
        out_shape=outs,
        in_specs=specs or [VMEM] * len(operands),
        out_specs=jax.tree.map(lambda _: VMEM, outs) if out_specs is None else out_specs,
        scratch_shapes=scratch,
        compiler_params=pltpu.CompilerParams(vmem_limit_bytes=VMEM_LIMIT),
        cost_estimate=pl.CostEstimate(flops=2**27, bytes_accessed=2**20, transcendentals=0),
    )(*operands)


def shape_of(*shape, dtype=BF16):
    return jax.ShapeDtypeStruct(shape, dtype)


def exchange(array):
    count = math.prod(AXES[a] for a in PEERS)
    blocks = array.reshape(count, array.shape[0] // count, array.shape[1])
    blocks = lax.all_to_all(blocks, PEERS, split_axis=0, concat_axis=0, tiled=True)
    return blocks.reshape(array.shape)


def shards(volume, x_frequency, y_frequency, measured, weights):
    x_local, y_local, length = volume.shape
    cells = x_local * y_local
    rows = cells * length // LANES
    planes, angles, kx_count = x_frequency.shape
    ky_count = y_frequency.shape[2]
    forward_scale = 1.0 / math.sqrt(cells * math.prod(AXES.values()))
    back_scale = 1.0 / math.sqrt(angles * kx_count * ky_count)
    columns = volume.reshape(cells, length)
    forward = column_table(length, 1.0 / math.sqrt(length))
    inverse = column_table(length, 1.0 / math.sqrt(planes))

    sending, own, x_table, y_table = local_call(
        start_kernel,
        (
            shape_of(rows, LANES),
            shape_of(24, LANES, dtype=F32),
            shape_of(PLANES * 32, 2 * LANES),
            shape_of(PLANES, 2 * LANES, 2 * LANES),
        ),
        (
            pin(x_frequency.transpose(1, 2, 0).reshape(angles * kx_count, planes)),
            pin(y_frequency.transpose(1, 2, 0).reshape(angles * ky_count, planes)),
            pin(columns),
            pin(jnp.asarray(forward)),
            pin(measured[0]),
            pin(weights[0]),
        ),
        [
            pltpu.VMEM((angles * kx_count, planes), jnp.int32),
            pltpu.VMEM((angles * ky_count, planes), jnp.int32),
            pltpu.VMEM((cells, length), BF16),
            pltpu.VMEM((length, length), BF16),
            pltpu.VMEM(measured.shape[1:], F32),
            pltpu.VMEM(weights.shape[1:], F32),
            pltpu.VMEM((planes, LANES), F32),
            pltpu.SemaphoreType.DMA((6,)),
        ],
        [HBM] * 6,
    )
    received = exchange(sending)
    total = local_call(
        functools.partial(predict_kernel, forward_scale),
        shape_of(PLANES, 24, LANES, dtype=F32),
        (received, y_table, x_table, own),
    )
    total = total + lax.ppermute(total, "c", SWAP)
    other = lax.ppermute(total.astype(BF16), "yh", SWAP)
    misfit, sending = local_call(
        functools.partial(spread_kernel, back_scale),
        (shape_of(angles * kx_count, LANES, dtype=F32), shape_of(rows, LANES)),
        (total, other, y_table, x_table),
    )
    received = exchange(sending)
    updated = local_call(
        update_kernel,
        shape_of(cells, length),
        (received, columns, inverse),
        [pltpu.VMEM((cells, length), BF16), pltpu.SemaphoreType.DMA((2,))],
        out_specs=ANY,
    )
    return (updated.reshape(volume.shape), misfit.reshape(measured.shape))


def solution(mesh):
    fine = Mesh(mesh.devices.reshape(tuple(AXES.values())), tuple(AXES))
    placed = (
        P(ROWS, SLAB, None),
        P(),
        P(),
        P(SLAB + ROWS, None, None),
        P(SLAB + ROWS, None, None),
    )
    return jax.shard_map(
        shards,
        mesh=fine,
        in_specs=placed,
        out_specs=(P(ROWS, SLAB, None), P(SLAB + ROWS, None, None)),
        check_vma=False,
    )
```

```python
import functools
import math

import jax
import jax.numpy as jnp
import numpy as np
from jax import lax
from jax.experimental import pallas as pl
from jax.experimental.pallas import tpu as pltpu
from jax.sharding import Mesh
from jax.sharding import PartitionSpec as P

FINE = 4096
LANES = 128
VMEM_LIMIT = 12 * 2**20
F32 = jnp.float32
BF16 = jnp.bfloat16
AXES = {"yh": 2, "yl": 2, "zl": 4, "c": 2, "zh": 2, "x": 4}
SLAB = ("yh", "yl", "zl", "c")
ROWS = ("zh", "x")
PEERS = ("zl", "zh", "x", "yl")
TEAM = ("yh", "c")
PLANES = 4
SWAP = [(0, 1), (1, 0)]


def plane_of(at):
    number = 0
    for axis in SLAB + ROWS:
        number = number * AXES[axis] + at[axis]
    return number


def column_table(length, scale):
    grid = np.arange(length // 2).reshape([AXES[a] for a in SLAB + ROWS])
    order = grid.transpose([(SLAB + ROWS).index(a) for a in PEERS + TEAM]).reshape(-1)
    depths = np.arange(length, dtype=np.int64)
    angles = (order[:, None] * depths[None, :] % length) * (2.0 * math.pi / length)
    matrix = np.stack([np.cos(angles), -np.sin(angles)], axis=1) * scale
    return matrix.reshape(length, length).astype(np.float32).astype(BF16)


def cosine_of_turns(turns):
    part = turns - jnp.floor(turns + 0.5)
    angle = (0.25 - jnp.abs(part)) * (2.0 * math.pi)
    square = angle * angle
    series = -1.0 / 39916800.0
    for term in (362880.0, -5040.0, 120.0, -6.0):
        series = series * square + 1.0 / term
    return angle + angle * square * series


def phases(turns):
    return cosine_of_turns(turns), cosine_of_turns(turns + 0.25)


def product(left, right):
    return (
        left[0] * right[0] - left[1] * right[1],
        left[0] * right[1] + left[1] * right[0],
    )


def dot(left, right, left_dim, right_dim):
    dims = (((left_dim,), (right_dim,)), ((), ()))
    return lax.dot_general(left, right, dims, preferred_element_type=F32)


def iota(shape, axis):
    return lax.broadcasted_iota(jnp.int32, shape, axis)


def exchange_grains(blocks, axis, grain):
    size = blocks[0].shape[axis]
    place = iota(blocks[0].shape, axis) & (4 * grain - 1)
    low = place < 2 * grain
    even = (place & grain) == 0
    first = [None] * 4
    for i in (0, 1):
        a, b = blocks[i], blocks[i + 2]
        first[i] = jnp.where(low, a, pltpu.roll(b, 2 * grain, axis))
        first[i + 2] = jnp.where(low, pltpu.roll(a, size - 2 * grain, axis), b)
    last = [None] * 4
    for i in (0, 2):
        a, b = first[i], first[i + 1]
        last[i] = jnp.where(even, a, pltpu.roll(b, grain, axis))
        last[i + 1] = jnp.where(even, pltpu.roll(a, size - grain, axis), b)
    return last


def start_kernel(
    x_hbm,
    y_hbm,
    columns_hbm,
    forward_hbm,
    measured_hbm,
    weights_hbm,
    out_ref,
    own_ref,
    x_table_ref,
    y_table_ref,
    x_all,
    y_all,
    columns,
    forward,
    measured,
    weights,
    turned,
    sems,
):
    pairs = (
        (x_hbm, x_all),
        (y_hbm, y_all),
        (columns_hbm, columns),
        (forward_hbm, forward),
        (measured_hbm, measured),
        (weights_hbm, weights),
    )
    loads = [pltpu.make_async_copy(a, b, sems.at[i]) for i, (a, b) in enumerate(pairs)]
    for load in loads:
        load.start()
    at = {a: lax.axis_index(a) for a in SLAB + ROWS}
    lane = iota((16, LANES), 1)
    x_at = (lane >> 4 & 1) * 32 + (lane >> 1 & 3) * 8 + (lane >> 3 & 1) * 4 + (lane >> 5)
    x_at = x_at.astype(F32) * (1.0 / FINE)
    x_shift = (lane & 1).astype(F32) * 0.75
    row = iota((8, LANES), 0)
    y_in = row.astype(F32)
    y_middle = (row * 8).astype(F32)
    y_block = (row * 64 + at["yh"] * 512 + at["c"] * 32).astype(F32)
    plane = [plane_of({**at, "yh": p >> 1, "c": p & 1}) for p in range(PLANES)]
    for load in loads[:2]:
        load.wait()
    turned[...] = y_all[...].astype(F32).T
    x_own = x_all[...].astype(F32)
    lane_plane = iota(x_own.shape, 1)
    for p in range(PLANES):
        ky = (turned[pl.ds(plane[p], 1), :] + FINE / 2.0) * (1.0 / FINE)
        fine = phases(ky * y_in)
        middle = phases(ky * y_middle)
        coarse = phases(ky * y_block)
        inner = [product((middle[0][b : b + 1], middle[1][b : b + 1]), fine) for b in range(4)]
        inner = [jnp.concatenate([m[i] for m in inner], axis=0) for i in range(2)]
        for b in range(8):
            real, imag = product((coarse[0][b : b + 1], coarse[1][b : b + 1]), inner)
            y_table_ref[p, pl.ds(b * 32, 32), :LANES] = real.astype(BF16)
            y_table_ref[p, pl.ds(b * 32, 32), LANES:] = imag.astype(BF16)
        kx = jnp.sum(jnp.where(lane_plane == plane[p], x_own, 0.0), axis=1, keepdims=True)
        real, imag = phases((kx + FINE / 2.0) * x_at + x_shift)
        real, imag, back = real.astype(BF16), imag.astype(BF16), (-imag).astype(BF16)
        x_table_ref[pl.ds(32 * p, 16), :LANES] = real
        x_table_ref[pl.ds(32 * p, 16), LANES:] = back
        x_table_ref[pl.ds(32 * p + 16, 16), :LANES] = imag
        x_table_ref[pl.ds(32 * p + 16, 16), LANES:] = real
    for load in loads[2:]:
        load.wait()
    own_ref[:16] = measured[...]
    own_ref[16:, : LANES // 2] = weights[:8]
    own_ref[16:, LANES // 2 :] = weights[8:]
    spectrum = dot(forward[...], columns[...], 1, 1)
    near = spectrum[:, :LANES].reshape(-1, 8, LANES)
    far = spectrum[:, LANES:].reshape(-1, 8, LANES)
    out_ref[...] = jnp.concatenate([near, far], axis=1).reshape(out_ref.shape).astype(BF16)


def own_plane():
    return lax.axis_index("yh") * 2 + lax.axis_index("c")


def predict_kernel(scale, planes_ref, y_ref, x_ref, own_ref, out_ref):
    quarter = planes_ref.shape[0] // 4
    blocks = [planes_ref[pl.ds(g * quarter, quarter), :] for g in range(4)]
    blocks = exchange_grains(blocks, 1, 32)
    left = [[[], []] for _ in range(PLANES)]
    for q in range(4):
        rows = blocks[q].reshape(2, 4, 2, 16, LANES)
        for i in range(2):
            parts = exchange_grains([rows[:, x, i] for x in range(4)], 1, 2)
            for p in range(PLANES):
                left[p][i].append(parts[p].reshape(-1, LANES))
    near, far = [], []
    for p in range(PLANES):
        side = jnp.concatenate([jnp.concatenate(half, axis=0) for half in left[p]], axis=1)
        inner = dot(side, y_ref[p], 1, 0).astype(BF16)
        near.append(inner[:, :LANES])
        far.append(inner[:, LANES:])
    inner = jnp.concatenate(
        [jnp.concatenate(near, axis=1), jnp.concatenate(far, axis=1)], axis=0
    )
    everything = dot(x_ref[...], inner, 1, 0)
    first = iota((8, LANES), 1) < LANES // 2
    for p in range(PLANES):
        points = everything[32 * p : 32 * p + 32, LANES * p : LANES * p + LANES] * scale
        real, imag = points[:16], points[16:]
        out_ref[p, :8] = jnp.where(first, real[:8], pltpu.roll(imag[:8], 64, 1))
        out_ref[p, 8:16] = jnp.where(first, pltpu.roll(real[8:], 64, 1), imag[8:])
        out_ref[p, 16:] = jnp.zeros((8, LANES), F32)
    own = own_plane()
    out_ref[own, :16] = out_ref[own, :16] - own_ref[:16]
    out_ref[own, 16:] = own_ref[16:]


def spread_kernel(scale, sum_ref, other_ref, y_ref, x_ref, misfit_ref, out_ref):
    first = iota((8, LANES), 1) < LANES // 2

    def misfit_of(total):
        near, far, weight = total[:8], total[8:16], total[16:]
        crossed = pltpu.roll(weight, 64, 1)
        return (
            near * jnp.where(first, weight, crossed),
            far * jnp.where(first, crossed, weight),
        )

    zero = jnp.zeros((8, LANES), F32)
    lanes = []
    for p in range(PLANES):
        near, far = misfit_of(sum_ref[p] + other_ref[p].astype(F32))
        near, far = near * scale, far * scale
        spread = [
            jnp.where(first, near, zero),
            jnp.where(first, zero, pltpu.roll(far, 64, 1)),
            jnp.where(first, pltpu.roll(near, 64, 1), zero),
            jnp.where(first, zero, far),
        ]
        before, after = [zero] * 4 * p, [zero] * 4 * (PLANES - 1 - p)
        lanes.append(jnp.concatenate(before + spread + after, axis=0))
    everything = dot(x_ref[...], jnp.concatenate(lanes, axis=1).astype(BF16), 0, 0).astype(BF16)
    planes = []
    for p in range(PLANES):
        inner = everything[:, LANES * p : LANES * p + LANES]
        inner = jnp.concatenate([inner[:LANES], inner[LANES:]], axis=1)
        plane = dot(inner, y_ref[p], 1, 1).astype(BF16)
        planes.append(plane.reshape(4, 2, 16, 2 * LANES))
    blocks = []
    for q in range(4):
        rows = []
        for i in range(2):
            part = slice(i * LANES, i * LANES + LANES)
            parts = exchange_grains([planes[p][q, :, :, part] for p in range(PLANES)], 1, 2)
            rows.append(jnp.stack(parts, axis=1))
        blocks.append(jnp.stack(rows, axis=2).reshape(-1, LANES))
    blocks = exchange_grains(blocks, 1, 32)
    quarter = out_ref.shape[0] // 4
    for g in range(4):
        out_ref[pl.ds(g * quarter, quarter), :] = blocks[g]
    own = own_plane()
    near, far = misfit_of(sum_ref[own] + other_ref[own].astype(F32))
    misfit_ref[:8], misfit_ref[8:] = near, far


def update_kernel(planes_ref, columns_ref, table_ref, out_hbm, staged, sems):
    planes = planes_ref[...].astype(F32).reshape(-1, 2, 8, LANES)
    table = table_ref[...]
    stores = []
    for i in range(2):
        part = pl.ds(i * LANES, LANES)
        correction = dot(planes[:, i].reshape(-1, LANES).astype(BF16), table, 0, 0)
        staged[part, :] = (columns_ref[part, :].astype(F32) - 0.5 * correction).astype(BF16)
        stores.append(pltpu.make_async_copy(staged.at[part], out_hbm.at[part], sems.at[i]))
        stores[-1].start()
    for store in stores:
        store.wait()


VMEM = pl.BlockSpec(memory_space=pltpu.VMEM)
HBM = pl.BlockSpec(memory_space=pltpu.HBM)
ANY = pl.BlockSpec(memory_space=pl.ANY)


def pin(array):
    return pltpu.with_memory_space_constraint(array, pltpu.HBM)


def local_call(kernel, outs, operands, scratch=(), specs=None, out_specs=None, flags=None):
    return pl.pallas_call(
        kernel,
        out_shape=outs,
        in_specs=specs or [VMEM] * len(operands),
        out_specs=jax.tree.map(lambda _: VMEM, outs) if out_specs is None else out_specs,
        scratch_shapes=scratch,
        compiler_params=pltpu.CompilerParams(vmem_limit_bytes=VMEM_LIMIT, flags=flags),
        cost_estimate=pl.CostEstimate(flops=2**27, bytes_accessed=2**20, transcendentals=0),
    )(*operands)


def shape_of(*shape, dtype=BF16):
    return jax.ShapeDtypeStruct(shape, dtype)


def exchange(array):
    count = math.prod(AXES[a] for a in PEERS)
    blocks = array.reshape(count, array.shape[0] // count, array.shape[1])
    blocks = lax.all_to_all(blocks, PEERS, split_axis=0, concat_axis=0, tiled=True)
    return blocks.reshape(array.shape)


def shards(volume, x_frequency, y_frequency, measured, weights):
    x_local, y_local, length = volume.shape
    cells = x_local * y_local
    rows = cells * length // LANES
    planes, angles, kx_count = x_frequency.shape
    ky_count = y_frequency.shape[2]
    forward_scale = 1.0 / math.sqrt(cells * math.prod(AXES.values()))
    back_scale = 1.0 / math.sqrt(angles * kx_count * ky_count)
    columns = volume.reshape(cells, length)
    forward = column_table(length, 1.0 / math.sqrt(length))
    inverse = column_table(length, 1.0 / math.sqrt(planes))

    sending, own, x_table, y_table = local_call(
        start_kernel,
        (
            shape_of(rows, LANES),
            shape_of(24, LANES, dtype=F32),
            shape_of(PLANES * 32, 2 * LANES),
            shape_of(PLANES, 2 * LANES, 2 * LANES),
        ),
        (
            pin(x_frequency.transpose(1, 2, 0).reshape(angles * kx_count, planes)),
            pin(y_frequency.transpose(1, 2, 0).reshape(angles * ky_count, planes)),
            pin(columns),
            pin(jnp.asarray(forward)),
            pin(measured[0]),
            pin(weights[0]),
        ),
        [
            pltpu.VMEM((angles * kx_count, planes), jnp.int32),
            pltpu.VMEM((angles * ky_count, planes), jnp.int32),
            pltpu.VMEM((cells, length), BF16),
            pltpu.VMEM((length, length), BF16),
            pltpu.VMEM(measured.shape[1:], F32),
            pltpu.VMEM(weights.shape[1:], F32),
            pltpu.VMEM((planes, LANES), F32),
            pltpu.SemaphoreType.DMA((6,)),
        ],
        [HBM] * 6,
    )
    received = exchange(sending)
    total = local_call(
        functools.partial(predict_kernel, forward_scale),
        shape_of(PLANES, 24, LANES, dtype=F32),
        (received, y_table, x_table, own),
    )
    total = total + lax.ppermute(total, "c", SWAP)
    other = lax.ppermute(total.astype(BF16), "yh", SWAP)
    misfit, sending = local_call(
        functools.partial(spread_kernel, back_scale),
        (shape_of(angles * kx_count, LANES, dtype=F32), shape_of(rows, LANES)),
        (total, other, y_table, x_table),
    )
    received = exchange(sending)
    updated = local_call(
        update_kernel,
        shape_of(cells, length),
        (received, columns, inverse),
        [pltpu.VMEM((cells, length), BF16), pltpu.SemaphoreType.DMA((2,))],
        out_specs=ANY,
    )
    return (updated.reshape(volume.shape), misfit.reshape(measured.shape))


def solution(mesh):
    fine = Mesh(mesh.devices.reshape(tuple(AXES.values())), tuple(AXES))
    placed = (
        P(ROWS, SLAB, None),
        P(),
        P(),
        P(SLAB + ROWS, None, None),
        P(SLAB + ROWS, None, None),
    )
    return jax.shard_map(
        shards,
        mesh=fine,
        in_specs=placed,
        out_specs=(P(ROWS, SLAB, None), P(SLAB + ROWS, None, None)),
        check_vma=False,
    )
```

```python
import functools
import math

import jax
import jax.numpy as jnp
import numpy as np
from jax import lax
from jax.experimental import pallas as pl
from jax.experimental.pallas import tpu as pltpu
from jax.sharding import Mesh
from jax.sharding import PartitionSpec as P

FINE = 4096
LANES = 128
VMEM_LIMIT = 12 * 2**20
F32 = jnp.float32
BF16 = jnp.bfloat16
AXES = {"yh": 2, "yl": 2, "zl": 4, "c": 2, "zh": 2, "x": 4}
SLAB = ("yh", "yl", "zl", "c")
ROWS = ("zh", "x")
PEERS = ("zl", "zh", "x", "yl")
TEAM = ("yh", "c")
PLANES = 4
SWAP = [(0, 1), (1, 0)]


def plane_of(at):
    number = 0
    for axis in SLAB + ROWS:
        number = number * AXES[axis] + at[axis]
    return number


def column_table(length, scale):
    grid = np.arange(length // 2).reshape([AXES[a] for a in SLAB + ROWS])
    order = grid.transpose([(SLAB + ROWS).index(a) for a in PEERS + TEAM]).reshape(-1)
    depths = np.arange(length, dtype=np.int64)
    angles = (order[:, None] * depths[None, :] % length) * (2.0 * math.pi / length)
    matrix = np.stack([np.cos(angles), -np.sin(angles)], axis=1) * scale
    return matrix.reshape(length, length).astype(np.float32).astype(BF16)


def cosine_of_turns(turns):
    part = turns - jnp.floor(turns + 0.5)
    angle = (0.25 - jnp.abs(part)) * (2.0 * math.pi)
    square = angle * angle
    series = -1.0 / 39916800.0
    for term in (362880.0, -5040.0, 120.0, -6.0):
        series = series * square + 1.0 / term
    return angle + angle * square * series


def phases(turns):
    return cosine_of_turns(turns), cosine_of_turns(turns + 0.25)


def product(left, right):
    return (
        left[0] * right[0] - left[1] * right[1],
        left[0] * right[1] + left[1] * right[0],
    )


def dot(left, right, left_dim, right_dim):
    dims = (((left_dim,), (right_dim,)), ((), ()))
    return lax.dot_general(left, right, dims, preferred_element_type=F32)


def iota(shape, axis):
    return lax.broadcasted_iota(jnp.int32, shape, axis)


def exchange_grains(blocks, axis, grain):
    size = blocks[0].shape[axis]
    place = iota(blocks[0].shape, axis) & (4 * grain - 1)
    low = place < 2 * grain
    even = (place & grain) == 0
    first = [None] * 4
    for i in (0, 1):
        a, b = blocks[i], blocks[i + 2]
        first[i] = jnp.where(low, a, pltpu.roll(b, 2 * grain, axis))
        first[i + 2] = jnp.where(low, pltpu.roll(a, size - 2 * grain, axis), b)
    last = [None] * 4
    for i in (0, 2):
        a, b = first[i], first[i + 1]
        last[i] = jnp.where(even, a, pltpu.roll(b, grain, axis))
        last[i + 1] = jnp.where(even, pltpu.roll(a, size - grain, axis), b)
    return last


def start_kernel(
    x_hbm,
    y_hbm,
    columns_hbm,
    forward_hbm,
    measured_hbm,
    weights_hbm,
    out_ref,
    own_ref,
    x_table_ref,
    y_table_ref,
    x_all,
    y_all,
    columns,
    forward,
    measured,
    weights,
    turned,
    sems,
):
    pairs = (
        (x_hbm, x_all),
        (y_hbm, y_all),
        (columns_hbm, columns),
        (forward_hbm, forward),
        (measured_hbm, measured),
        (weights_hbm, weights),
    )
    loads = [pltpu.make_async_copy(a, b, sems.at[i]) for i, (a, b) in enumerate(pairs)]
    for load in loads:
        load.start()
    at = {a: lax.axis_index(a) for a in SLAB + ROWS}
    lane = iota((16, LANES), 1)
    x_at = (lane >> 4 & 1) * 32 + (lane >> 1 & 3) * 8 + (lane >> 3 & 1) * 4 + (lane >> 5)
    x_at = x_at.astype(F32) * (1.0 / FINE)
    x_shift = (lane & 1).astype(F32) * 0.75
    row = iota((8, LANES), 0)
    y_in = row.astype(F32)
    y_middle = (row * 8).astype(F32)
    y_block = (row * 64 + at["yh"] * 512 + at["c"] * 32).astype(F32)
    plane = [plane_of({**at, "yh": p >> 1, "c": p & 1}) for p in range(PLANES)]
    for load in loads[:2]:
        load.wait()
    turned[...] = y_all[...].astype(F32).T
    x_own = x_all[...].astype(F32)
    lane_plane = iota(x_own.shape, 1)
    def plane_tables(p):
        ky = (turned[pl.ds(plane[p], 1), :] + FINE / 2.0) * (1.0 / FINE)
        fine = phases(ky * y_in)
        middle = phases(ky * y_middle)
        coarse = phases(ky * y_block)
        inner = [product((middle[0][b : b + 1], middle[1][b : b + 1]), fine) for b in range(4)]
        inner = [jnp.concatenate([m[i] for m in inner], axis=0) for i in range(2)]
        for b in range(8):
            real, imag = product((coarse[0][b : b + 1], coarse[1][b : b + 1]), inner)
            y_table_ref[p, pl.ds(b * 32, 32), :LANES] = real.astype(BF16)
            y_table_ref[p, pl.ds(b * 32, 32), LANES:] = imag.astype(BF16)
        kx = jnp.sum(jnp.where(lane_plane == plane[p], x_own, 0.0), axis=1, keepdims=True)
        real, imag = phases((kx + FINE / 2.0) * x_at + x_shift)
        real, imag, back = real.astype(BF16), imag.astype(BF16), (-imag).astype(BF16)
        x_table_ref[pl.ds(32 * p, 16), :LANES] = real
        x_table_ref[pl.ds(32 * p, 16), LANES:] = back
        x_table_ref[pl.ds(32 * p + 16, 16), :LANES] = imag
        x_table_ref[pl.ds(32 * p + 16, 16), LANES:] = real

    for p in range(2):
        plane_tables(p)
    for load in loads[2:]:
        load.wait()
    own_ref[:16] = measured[...]
    own_ref[16:, : LANES // 2] = weights[:8]
    own_ref[16:, LANES // 2 :] = weights[8:]
    for p in range(2, PLANES):
        plane_tables(p)
    spectrum = dot(forward[...], columns[...], 1, 1)
    near = spectrum[:, :LANES].reshape(-1, 8, LANES)
    far = spectrum[:, LANES:].reshape(-1, 8, LANES)
    out_ref[...] = jnp.concatenate([near, far], axis=1).reshape(out_ref.shape).astype(BF16)


def own_plane():
    return lax.axis_index("yh") * 2 + lax.axis_index("c")


def predict_kernel(scale, planes_ref, y_ref, x_ref, own_ref, out_ref):
    quarter = planes_ref.shape[0] // 4
    blocks = [planes_ref[pl.ds(g * quarter, quarter), :] for g in range(4)]
    blocks = exchange_grains(blocks, 1, 32)
    left = [[[], []] for _ in range(PLANES)]
    for q in range(4):
        rows = blocks[q].reshape(2, 4, 2, 16, LANES)
        for i in range(2):
            parts = exchange_grains([rows[:, x, i] for x in range(4)], 1, 2)
            for p in range(PLANES):
                left[p][i].append(parts[p].reshape(-1, LANES))
    near, far = [], []
    for p in range(PLANES):
        side = jnp.concatenate([jnp.concatenate(half, axis=0) for half in left[p]], axis=1)
        inner = dot(side, y_ref[p], 1, 0).astype(BF16)
        near.append(inner[:, :LANES])
        far.append(inner[:, LANES:])
    inner = jnp.concatenate(
        [jnp.concatenate(near, axis=1), jnp.concatenate(far, axis=1)], axis=0
    )
    everything = dot(x_ref[...], inner, 1, 0)
    first = iota((8, LANES), 1) < LANES // 2
    for p in range(PLANES):
        points = everything[32 * p : 32 * p + 32, LANES * p : LANES * p + LANES] * scale
        real, imag = points[:16], points[16:]
        out_ref[p, :8] = jnp.where(first, real[:8], pltpu.roll(imag[:8], 64, 1))
        out_ref[p, 8:16] = jnp.where(first, pltpu.roll(real[8:], 64, 1), imag[8:])
        out_ref[p, 16:] = jnp.zeros((8, LANES), F32)
    own = own_plane()
    out_ref[own, :16] = out_ref[own, :16] - own_ref[:16]
    out_ref[own, 16:] = own_ref[16:]


def spread_kernel(scale, sum_ref, other_ref, y_ref, x_ref, misfit_ref, out_ref):
    first = iota((8, LANES), 1) < LANES // 2

    def misfit_of(total):
        near, far, weight = total[:8], total[8:16], total[16:]
        crossed = pltpu.roll(weight, 64, 1)
        return (
            near * jnp.where(first, weight, crossed),
            far * jnp.where(first, crossed, weight),
        )

    zero = jnp.zeros((8, LANES), F32)
    lanes = []
    for p in range(PLANES):
        near, far = misfit_of(sum_ref[p] + other_ref[p].astype(F32))
        near, far = near * scale, far * scale
        spread = [
            jnp.where(first, near, zero),
            jnp.where(first, zero, pltpu.roll(far, 64, 1)),
            jnp.where(first, pltpu.roll(near, 64, 1), zero),
            jnp.where(first, zero, far),
        ]
        before, after = [zero] * 4 * p, [zero] * 4 * (PLANES - 1 - p)
        lanes.append(jnp.concatenate(before + spread + after, axis=0))
    everything = dot(x_ref[...], jnp.concatenate(lanes, axis=1).astype(BF16), 0, 0).astype(BF16)
    planes = []
    for p in range(PLANES):
        inner = everything[:, LANES * p : LANES * p + LANES]
        inner = jnp.concatenate([inner[:LANES], inner[LANES:]], axis=1)
        plane = dot(inner, y_ref[p], 1, 1).astype(BF16)
        planes.append(plane.reshape(4, 2, 16, 2 * LANES))
    blocks = []
    for q in range(4):
        rows = []
        for i in range(2):
            part = slice(i * LANES, i * LANES + LANES)
            parts = exchange_grains([planes[p][q, :, :, part] for p in range(PLANES)], 1, 2)
            rows.append(jnp.stack(parts, axis=1))
        blocks.append(jnp.stack(rows, axis=2).reshape(-1, LANES))
    blocks = exchange_grains(blocks, 1, 32)
    quarter = out_ref.shape[0] // 4
    for g in range(4):
        out_ref[pl.ds(g * quarter, quarter), :] = blocks[g]
    own = own_plane()
    near, far = misfit_of(sum_ref[own] + other_ref[own].astype(F32))
    misfit_ref[:8], misfit_ref[8:] = near, far


def update_kernel(planes_ref, columns_ref, table_ref, out_hbm, staged, sems):
    planes = planes_ref[...].astype(F32).reshape(-1, 2, 8, LANES)
    table = table_ref[...]
    stores = []
    for i in range(2):
        part = pl.ds(i * LANES, LANES)
        correction = dot(planes[:, i].reshape(-1, LANES).astype(BF16), table, 0, 0)
        staged[part, :] = (columns_ref[part, :].astype(F32) - 0.5 * correction).astype(BF16)
        stores.append(pltpu.make_async_copy(staged.at[part], out_hbm.at[part], sems.at[i]))
        stores[-1].start()
    for store in stores:
        store.wait()


VMEM = pl.BlockSpec(memory_space=pltpu.VMEM)
HBM = pl.BlockSpec(memory_space=pltpu.HBM)
ANY = pl.BlockSpec(memory_space=pl.ANY)


def pin(array):
    return pltpu.with_memory_space_constraint(array, pltpu.HBM)


def local_call(kernel, outs, operands, scratch=(), specs=None, out_specs=None, flags=None):
    return pl.pallas_call(
        kernel,
        out_shape=outs,
        in_specs=specs or [VMEM] * len(operands),
        out_specs=jax.tree.map(lambda _: VMEM, outs) if out_specs is None else out_specs,
        scratch_shapes=scratch,
        compiler_params=pltpu.CompilerParams(vmem_limit_bytes=VMEM_LIMIT, flags=flags),
        cost_estimate=pl.CostEstimate(flops=2**27, bytes_accessed=2**20, transcendentals=0),
    )(*operands)


def shape_of(*shape, dtype=BF16):
    return jax.ShapeDtypeStruct(shape, dtype)


def exchange(array):
    count = math.prod(AXES[a] for a in PEERS)
    blocks = array.reshape(count, array.shape[0] // count, array.shape[1])
    blocks = lax.all_to_all(blocks, PEERS, split_axis=0, concat_axis=0, tiled=True)
    return blocks.reshape(array.shape)


def shards(volume, x_frequency, y_frequency, measured, weights):
    x_local, y_local, length = volume.shape
    cells = x_local * y_local
    rows = cells * length // LANES
    planes, angles, kx_count = x_frequency.shape
    ky_count = y_frequency.shape[2]
    forward_scale = 1.0 / math.sqrt(cells * math.prod(AXES.values()))
    back_scale = 1.0 / math.sqrt(angles * kx_count * ky_count)
    columns = volume.reshape(cells, length)
    forward = column_table(length, 1.0 / math.sqrt(length))
    inverse = column_table(length, 1.0 / math.sqrt(planes))

    sending, own, x_table, y_table = local_call(
        start_kernel,
        (
            shape_of(rows, LANES),
            shape_of(24, LANES, dtype=F32),
            shape_of(PLANES * 32, 2 * LANES),
            shape_of(PLANES, 2 * LANES, 2 * LANES),
        ),
        (
            pin(x_frequency.transpose(1, 2, 0).reshape(angles * kx_count, planes)),
            pin(y_frequency.transpose(1, 2, 0).reshape(angles * ky_count, planes)),
            pin(columns),
            pin(jnp.asarray(forward)),
            pin(measured[0]),
            pin(weights[0]),
        ),
        [
            pltpu.VMEM((angles * kx_count, planes), jnp.int32),
            pltpu.VMEM((angles * ky_count, planes), jnp.int32),
            pltpu.VMEM((cells, length), BF16),
            pltpu.VMEM((length, length), BF16),
            pltpu.VMEM(measured.shape[1:], F32),
            pltpu.VMEM(weights.shape[1:], F32),
            pltpu.VMEM((planes, LANES), F32),
            pltpu.SemaphoreType.DMA((6,)),
        ],
        [HBM] * 6,
    )
    received = exchange(sending)
    total = local_call(
        functools.partial(predict_kernel, forward_scale),
        shape_of(PLANES, 24, LANES, dtype=F32),
        (received, y_table, x_table, own),
    )
    total = total + lax.ppermute(total, "c", SWAP)
    other = lax.ppermute(total.astype(BF16), "yh", SWAP)
    misfit, sending = local_call(
        functools.partial(spread_kernel, back_scale),
        (shape_of(angles * kx_count, LANES, dtype=F32), shape_of(rows, LANES)),
        (total, other, y_table, x_table),
    )
    received = exchange(sending)
    updated = local_call(
        update_kernel,
        shape_of(cells, length),
        (received, columns, inverse),
        [pltpu.VMEM((cells, length), BF16), pltpu.SemaphoreType.DMA((2,))],
        out_specs=ANY,
    )
    return (updated.reshape(volume.shape), misfit.reshape(measured.shape))


def solution(mesh):
    fine = Mesh(mesh.devices.reshape(tuple(AXES.values())), tuple(AXES))
    placed = (
        P(ROWS, SLAB, None),
        P(),
        P(),
        P(SLAB + ROWS, None, None),
        P(SLAB + ROWS, None, None),
    )
    return jax.shard_map(
        shards,
        mesh=fine,
        in_specs=placed,
        out_specs=(P(ROWS, SLAB, None), P(SLAB + ROWS, None, None)),
        check_vma=False,
    )
```

```python
import functools
import math

import jax
import jax.numpy as jnp
import numpy as np
from jax import lax
from jax.experimental import pallas as pl
from jax.experimental.pallas import tpu as pltpu
from jax.sharding import Mesh
from jax.sharding import PartitionSpec as P

FINE = 4096
LANES = 128
VMEM_LIMIT = 12 * 2**20
F32 = jnp.float32
BF16 = jnp.bfloat16
AXES = {"yh": 2, "yl": 2, "zl": 4, "c": 2, "zh": 2, "x": 4}
SLAB = ("yh", "yl", "zl", "c")
ROWS = ("zh", "x")
PEERS = ("zl", "zh", "x", "yl")
TEAM = ("yh", "c")
PLANES = 4
SWAP = [(0, 1), (1, 0)]


def plane_of(at):
    number = 0
    for axis in SLAB + ROWS:
        number = number * AXES[axis] + at[axis]
    return number


def column_table(length, scale):
    grid = np.arange(length // 2).reshape([AXES[a] for a in SLAB + ROWS])
    order = grid.transpose([(SLAB + ROWS).index(a) for a in PEERS + TEAM]).reshape(-1)
    depths = np.arange(length, dtype=np.int64)
    angles = (order[:, None] * depths[None, :] % length) * (2.0 * math.pi / length)
    matrix = np.stack([np.cos(angles), -np.sin(angles)], axis=1) * scale
    return matrix.reshape(length, length).astype(np.float32).astype(BF16)


def cosine_of_turns(turns):
    part = turns - jnp.floor(turns + 0.5)
    angle = (0.25 - jnp.abs(part)) * (2.0 * math.pi)
    square = angle * angle
    series = -1.0 / 39916800.0
    for term in (362880.0, -5040.0, 120.0, -6.0):
        series = series * square + 1.0 / term
    return angle + angle * square * series


def phases(turns):
    return cosine_of_turns(turns), cosine_of_turns(turns + 0.25)


def product(left, right):
    return (
        left[0] * right[0] - left[1] * right[1],
        left[0] * right[1] + left[1] * right[0],
    )


def dot(left, right, left_dim, right_dim):
    dims = (((left_dim,), (right_dim,)), ((), ()))
    return lax.dot_general(left, right, dims, preferred_element_type=F32)


def iota(shape, axis):
    return lax.broadcasted_iota(jnp.int32, shape, axis)


def exchange_grains(blocks, axis, grain):
    size = blocks[0].shape[axis]
    place = iota(blocks[0].shape, axis) & (4 * grain - 1)
    low = place < 2 * grain
    even = (place & grain) == 0
    first = [None] * 4
    for i in (0, 1):
        a, b = blocks[i], blocks[i + 2]
        first[i] = jnp.where(low, a, pltpu.roll(b, 2 * grain, axis))
        first[i + 2] = jnp.where(low, pltpu.roll(a, size - 2 * grain, axis), b)
    last = [None] * 4
    for i in (0, 2):
        a, b = first[i], first[i + 1]
        last[i] = jnp.where(even, a, pltpu.roll(b, grain, axis))
        last[i + 1] = jnp.where(even, pltpu.roll(a, size - grain, axis), b)
    return last


def start_kernel(
    x_hbm,
    y_hbm,
    columns_hbm,
    forward_hbm,
    measured_hbm,
    weights_hbm,
    out_ref,
    own_ref,
    x_table_ref,
    y_table_ref,
    x_all,
    y_all,
    columns,
    forward,
    measured,
    weights,
    turned,
    sems,
):
    pairs = (
        (x_hbm, x_all),
        (y_hbm, y_all),
        (columns_hbm, columns),
        (forward_hbm, forward),
        (measured_hbm, measured),
        (weights_hbm, weights),
    )
    loads = [pltpu.make_async_copy(a, b, sems.at[i]) for i, (a, b) in enumerate(pairs)]
    for load in loads:
        load.start()
    at = {a: lax.axis_index(a) for a in SLAB + ROWS}
    lane = iota((16, LANES), 1)
    x_at = (lane >> 4 & 1) * 32 + (lane >> 1 & 3) * 8 + (lane >> 3 & 1) * 4 + (lane >> 5)
    x_at = x_at.astype(F32) * (1.0 / FINE)
    x_shift = (lane & 1).astype(F32) * 0.75
    row = iota((8, LANES), 0)
    y_in = row.astype(F32)
    y_middle = (row * 8).astype(F32)
    y_block = (row * 64 + at["yh"] * 512 + at["c"] * 32).astype(F32)
    plane = [plane_of({**at, "yh": p >> 1, "c": p & 1}) for p in range(PLANES)]
    for load in loads[:2]:
        load.wait()
    turned[...] = y_all[...].astype(F32).T
    x_own = x_all[...].astype(F32)
    lane_plane = iota(x_own.shape, 1)
    def plane_tables(p):
        ky = (turned[pl.ds(plane[p], 1), :] + FINE / 2.0) * (1.0 / FINE)
        fine = phases(ky * y_in)
        middle = phases(ky * y_middle)
        coarse = phases(ky * y_block)
        inner = [product((middle[0][b : b + 1], middle[1][b : b + 1]), fine) for b in range(4)]
        inner = [jnp.concatenate([m[i] for m in inner], axis=0) for i in range(2)]
        for b in range(8):
            real, imag = product((coarse[0][b : b + 1], coarse[1][b : b + 1]), inner)
            y_table_ref[p, pl.ds(b * 32, 32), :LANES] = real.astype(BF16)
            y_table_ref[p, pl.ds(b * 32, 32), LANES:] = imag.astype(BF16)
        kx = jnp.sum(jnp.where(lane_plane == plane[p], x_own, 0.0), axis=1, keepdims=True)
        real, imag = phases((kx + FINE / 2.0) * x_at + x_shift)
        real, imag, back = real.astype(BF16), imag.astype(BF16), (-imag).astype(BF16)
        x_table_ref[pl.ds(32 * p, 16), :LANES] = real
        x_table_ref[pl.ds(32 * p, 16), LANES:] = back
        x_table_ref[pl.ds(32 * p + 16, 16), :LANES] = imag
        x_table_ref[pl.ds(32 * p + 16, 16), LANES:] = real

    for p in range(2):
        plane_tables(p)
    for load in loads[2:]:
        load.wait()
    own_ref[:16] = measured[...]
    own_ref[16:, : LANES // 2] = weights[:8]
    own_ref[16:, LANES // 2 :] = weights[8:]
    for p in range(2, PLANES):
        plane_tables(p)
    spectrum = dot(forward[...], columns[...], 1, 1)
    near = spectrum[:, :LANES].reshape(-1, 8, LANES)
    far = spectrum[:, LANES:].reshape(-1, 8, LANES)
    out_ref[...] = jnp.concatenate([near, far], axis=1).reshape(out_ref.shape).astype(BF16)


def own_plane():
    return lax.axis_index("yh") * 2 + lax.axis_index("c")


def predict_kernel(scale, planes_ref, y_ref, x_ref, own_ref, out_ref):
    quarter = planes_ref.shape[0] // 4
    blocks = [planes_ref[pl.ds(g * quarter, quarter), :] for g in range(4)]
    blocks = exchange_grains(blocks, 1, 32)
    left = [[[], []] for _ in range(PLANES)]
    for q in range(4):
        rows = blocks[q].reshape(2, 4, 2, 16, LANES)
        for i in range(2):
            parts = exchange_grains([rows[:, x, i] for x in range(4)], 1, 2)
            for p in range(PLANES):
                left[p][i].append(parts[p].reshape(-1, LANES))
    near, far = [], []
    for p in range(PLANES):
        side = jnp.concatenate([jnp.concatenate(half, axis=0) for half in left[p]], axis=1)
        inner = dot(side, y_ref[p], 1, 0).astype(BF16)
        near.append(inner[:, :LANES])
        far.append(inner[:, LANES:])
    inner = jnp.concatenate(
        [jnp.concatenate(near, axis=1), jnp.concatenate(far, axis=1)], axis=0
    )
    everything = dot(x_ref[...], inner, 1, 0)
    first = iota((8, LANES), 1) < LANES // 2
    for p in range(PLANES):
        points = everything[32 * p : 32 * p + 32, LANES * p : LANES * p + LANES] * scale
        real, imag = points[:16], points[16:]
        out_ref[p, :8] = jnp.where(first, real[:8], pltpu.roll(imag[:8], 64, 1))
        out_ref[p, 8:16] = jnp.where(first, pltpu.roll(real[8:], 64, 1), imag[8:])
        out_ref[p, 16:] = jnp.zeros((8, LANES), F32)
    own = own_plane()
    out_ref[own, :16] = out_ref[own, :16] - own_ref[:16]
    out_ref[own, 16:] = own_ref[16:]


def spread_kernel(scale, sum_ref, other_ref, y_ref, x_ref, misfit_ref, out_ref):
    first = iota((8, LANES), 1) < LANES // 2

    def misfit_of(total):
        near, far, weight = total[:8], total[8:16], total[16:]
        crossed = pltpu.roll(weight, 64, 1)
        return (
            near * jnp.where(first, weight, crossed),
            far * jnp.where(first, crossed, weight),
        )

    zero = jnp.zeros((8, LANES), F32)
    lanes = []
    for p in range(PLANES):
        near, far = misfit_of(sum_ref[p] + other_ref[p].astype(F32))
        near, far = near * scale, far * scale
        spread = [
            jnp.where(first, near, zero),
            jnp.where(first, zero, pltpu.roll(far, 64, 1)),
            jnp.where(first, pltpu.roll(near, 64, 1), zero),
            jnp.where(first, zero, far),
        ]
        before, after = [zero] * 4 * p, [zero] * 4 * (PLANES - 1 - p)
        lanes.append(jnp.concatenate(before + spread + after, axis=0))
    everything = dot(x_ref[...], jnp.concatenate(lanes, axis=1).astype(BF16), 0, 0).astype(BF16)
    planes = []
    for p in range(PLANES):
        inner = everything[:, LANES * p : LANES * p + LANES]
        inner = jnp.concatenate([inner[:LANES], inner[LANES:]], axis=1)
        plane = dot(inner, y_ref[p], 1, 1).astype(BF16)
        planes.append(plane.reshape(4, 2, 16, 2 * LANES))
    blocks = []
    for q in range(4):
        rows = []
        for i in range(2):
            part = slice(i * LANES, i * LANES + LANES)
            parts = exchange_grains([planes[p][q, :, :, part] for p in range(PLANES)], 1, 2)
            rows.append(jnp.stack(parts, axis=1))
        blocks.append(jnp.stack(rows, axis=2).reshape(-1, LANES))
    blocks = exchange_grains(blocks, 1, 32)
    quarter = out_ref.shape[0] // 4
    for g in range(4):
        out_ref[pl.ds(g * quarter, quarter), :] = blocks[g]
    own = own_plane()
    near, far = misfit_of(sum_ref[own] + other_ref[own].astype(F32))
    misfit_ref[:8], misfit_ref[8:] = near, far


def update_kernel(planes_ref, columns_ref, table_ref, out_hbm, staged, sems):
    planes = planes_ref[...].astype(F32).reshape(-1, 2, 8, LANES)
    table = table_ref[...]
    stores = []
    for i in range(2):
        part = pl.ds(i * LANES, LANES)
        correction = dot(planes[:, i].reshape(-1, LANES).astype(BF16), table, 0, 0)
        staged[part, :] = (columns_ref[part, :].astype(F32) - 0.5 * correction).astype(BF16)
        stores.append(pltpu.make_async_copy(staged.at[part], out_hbm.at[part], sems.at[i]))
        stores[-1].start()
    for store in stores:
        store.wait()


VMEM = pl.BlockSpec(memory_space=pltpu.VMEM)
HBM = pl.BlockSpec(memory_space=pltpu.HBM)
ANY = pl.BlockSpec(memory_space=pl.ANY)


def pin(array):
    return pltpu.with_memory_space_constraint(array, pltpu.HBM)


def local_call(kernel, outs, operands, scratch=(), specs=None, out_specs=None, flags=None):
    return pl.pallas_call(
        kernel,
        out_shape=outs,
        in_specs=specs or [VMEM] * len(operands),
        out_specs=jax.tree.map(lambda _: VMEM, outs) if out_specs is None else out_specs,
        scratch_shapes=scratch,
        compiler_params=pltpu.CompilerParams(vmem_limit_bytes=VMEM_LIMIT, flags=flags),
        cost_estimate=pl.CostEstimate(flops=2**27, bytes_accessed=2**20, transcendentals=0),
    )(*operands)


def shape_of(*shape, dtype=BF16):
    return jax.ShapeDtypeStruct(shape, dtype)


def exchange(array):
    count = math.prod(AXES[a] for a in PEERS)
    blocks = array.reshape(count, array.shape[0] // count, array.shape[1])
    blocks = lax.all_to_all(blocks, PEERS, split_axis=0, concat_axis=0, tiled=True)
    return blocks.reshape(array.shape)


def shards(volume, x_frequency, y_frequency, measured, weights):
    x_local, y_local, length = volume.shape
    cells = x_local * y_local
    rows = cells * length // LANES
    planes, angles, kx_count = x_frequency.shape
    ky_count = y_frequency.shape[2]
    forward_scale = 1.0 / math.sqrt(cells * math.prod(AXES.values()))
    back_scale = 1.0 / math.sqrt(angles * kx_count * ky_count)
    columns = volume.reshape(cells, length)
    forward = column_table(length, 1.0 / math.sqrt(length))
    inverse = column_table(length, 1.0 / math.sqrt(planes))

    sending, own, x_table, y_table = local_call(
        start_kernel,
        (
            shape_of(rows, LANES),
            shape_of(24, LANES, dtype=F32),
            shape_of(PLANES * 32, 2 * LANES),
            shape_of(PLANES, 2 * LANES, 2 * LANES),
        ),
        (
            pin(x_frequency.transpose(1, 2, 0).reshape(angles * kx_count, planes)),
            pin(y_frequency.transpose(1, 2, 0).reshape(angles * ky_count, planes)),
            pin(columns),
            pin(jnp.asarray(forward)),
            pin(measured[0]),
            pin(weights[0]),
        ),
        [
            pltpu.VMEM((angles * kx_count, planes), jnp.int32),
            pltpu.VMEM((angles * ky_count, planes), jnp.int32),
            pltpu.VMEM((cells, length), BF16),
            pltpu.VMEM((length, length), BF16),
            pltpu.VMEM(measured.shape[1:], F32),
            pltpu.VMEM(weights.shape[1:], F32),
            pltpu.VMEM((planes, LANES), F32),
            pltpu.SemaphoreType.DMA((6,)),
        ],
        [HBM] * 6,
    )
    received = exchange(sending)
    total = local_call(
        functools.partial(predict_kernel, forward_scale),
        shape_of(PLANES, 24, LANES, dtype=F32),
        (received, y_table, x_table, own),
    )
    total = total + lax.ppermute(total.astype(BF16), "c", SWAP).astype(F32)
    other = lax.ppermute(total.astype(BF16), "yh", SWAP)
    misfit, sending = local_call(
        functools.partial(spread_kernel, back_scale),
        (shape_of(angles * kx_count, LANES, dtype=F32), shape_of(rows, LANES)),
        (total, other, y_table, x_table),
    )
    received = exchange(sending)
    updated = local_call(
        update_kernel,
        shape_of(cells, length),
        (received, columns, inverse),
        [pltpu.VMEM((cells, length), BF16), pltpu.SemaphoreType.DMA((2,))],
        out_specs=ANY,
    )
    return (updated.reshape(volume.shape), misfit.reshape(measured.shape))


def solution(mesh):
    fine = Mesh(mesh.devices.reshape(tuple(AXES.values())), tuple(AXES))
    placed = (
        P(ROWS, SLAB, None),
        P(),
        P(),
        P(SLAB + ROWS, None, None),
        P(SLAB + ROWS, None, None),
    )
    return jax.shard_map(
        shards,
        mesh=fine,
        in_specs=placed,
        out_specs=(P(ROWS, SLAB, None), P(SLAB + ROWS, None, None)),
        check_vma=False,
    )
```
